512 devices in a mesh: ctx: 128 (over y, z, core), head: 4 (over x).
Axes of the slice: x: 4, y: 8, z: 8, core: 2. Of those that a mesh axis runs over, the one named last changes fastest.
Arguments:
- queries: bfloat16 [65536, 8192], P(('ctx', 'head')), may hold values from -6 to 6
- key_rows: bfloat16 [65536, 1024], P(('ctx', 'head')), may hold values from -6 to 6
- value_rows: bfloat16 [65536, 1024], P(('ctx', 'head')), may hold values from -6 to 6
- doc_lengths: int32 [128], replicated, may hold values from 1 to 384, 32768 in all
Outputs:
- attended: bfloat16 [65536, 8192], P('ctx', 'head')
The draws below stay inside these ranges and needn't reach their ends.
All inputs are finite; a program needn't handle non-finite values.
Results may differ from the reference program's by a relative error of at most 0.0036.
Values may be sent and summed in bfloat16 or wider, within the bound.
No kernel may reach another device: no remote copies, remote signals or barrier semaphores. Data moves between devices by JAX's collectives and lax.ppermute only.
A program may use at most 64 MiB of HBM per device.

```python
import math
import jax
import jax.numpy as jnp
import numpy as np
from jax import lax

HEAD_DIM = 128
QHEADS = 64
KVHEADS = 8
REACH = 3
STRETCH = 256
SEQ = 65536
DOCS = 128
MOST_DOC = 768
N_CTX = 128


def draw_queries(key, part):
    width = QHEADS * HEAD_DIM
    result = jnp.clip(jax.random.normal(jax.random.fold_in(key, 11), (SEQ, width)), -6.0, 6.0)
    return result.astype(jnp.bfloat16)


def draw_key_rows(key, part):
    width = KVHEADS * HEAD_DIM
    result = jnp.clip(jax.random.normal(jax.random.fold_in(key, 12), (SEQ, width)), -6.0, 6.0)
    return result.astype(jnp.bfloat16)


def levels(own_key, extent, shards, least, high):
    loudness, own = 1.0, jax.random.fold_in(own_key, 6)
    for axis_at, parts in shards:
        draws = jnp.exp(jax.random.uniform(jax.random.fold_in(own, axis_at), (parts,), jnp.float32, least / len(shards), high / len(shards)))
        loudness = loudness * jnp.repeat(draws, extent[axis_at] // parts).reshape([-1 if axis == axis_at else 1 for axis in range(len(extent))])
    return loudness


def profile(amount, total, limit, skew):
    loads = [(1 << 20) // math.isqrt(standing ** skew) + 1 for standing in range(2, amount + 1)]
    spare, counts = total - limit - (amount - 1), [1] * (amount - 1)
    while spare > 0:
        free = [i for i in range(amount - 1) if counts[i] < limit]
        pool, budget = sum([loads[i] for i in free]), spare
        for i in free:
            extra = min(limit - counts[i], max(1, budget * loads[i] // pool), spare)
            counts[i] = counts[i] + extra
            spare = spare - extra
    return np.array([limit] + counts)


def ragged(own_key, number_of, total, most, skew):
    if number_of == 2:
        one = jax.random.randint(own_key, (), max(1, total - most), min(most, total - 1) + 1)
        return jnp.stack([one, total - one])
    tallies = jnp.asarray(profile(number_of, total, most, skew), jnp.int32)
    couples = (number_of - 1) // 2
    giver, taker = tallies[1:1 + 2 * couples:2], tallies[2:2 + 2 * couples:2]
    margin = jnp.minimum(giver - 1, most - taker)
    shifted = jax.random.randint(jax.random.fold_in(own_key, 1), (couples,), 0, 1 << 20) % (margin + 1)
    tallies = tallies.at[1:1 + 2 * couples:2].set(giver - shifted).at[2:2 + 2 * couples:2].set(taker + shifted)
    return tallies[jax.random.permutation(jax.random.fold_in(own_key, 2), number_of)]


def noise(own_key, extent, deviation, bound, shards=(), kind=jnp.bfloat16):
    factor_of = levels(own_key, extent, shards, -0.22, 0.18) if shards else 1.0
    entries = jax.random.normal(own_key, extent, jnp.float32) * deviation * factor_of
    return jnp.minimum(jnp.maximum(entries, -bound), bound).astype(kind)


def setup_inputs(seed: int = 0) -> dict:
    keys = jax.random.split(jax.random.key(seed), 5)
    queries = draw_queries(jax.random.fold_in(keys[4], 71), 0)
    key_rows = draw_key_rows(jax.random.fold_in(keys[4], 71), 0)
    value_rows = noise(keys[2], (SEQ, KVHEADS * HEAD_DIM), 1.0, 6.0, ((0, 512),))
    doc_lengths = ragged(keys[3], DOCS, SEQ // 2, MOST_DOC // 2, 2).astype(jnp.int32)
    return {"queries": queries, "key_rows": key_rows, "value_rows": value_rows, "doc_lengths": doc_lengths}


def natural_order(matrix):
    blocks = matrix.reshape(N_CTX, 2, STRETCH, matrix.shape[1])
    return jnp.concatenate([blocks[:, 0], jnp.flip(blocks[:, 1], axis=0)], axis=0)


def doc_of(positions, starts):
    marks = (starts[None, :] <= positions[:, None]).astype(jnp.int32)
    return jnp.sum(marks, axis=1).astype(jnp.int32) - 1


def reference(queries, key_rows, value_rows, doc_lengths):
    sizes = doc_lengths.astype(jnp.int32) * 2
    starts = (jnp.cumsum(sizes) - sizes).astype(jnp.int32)
    query_nat = natural_order(queries)
    key_nat = natural_order(key_rows)
    value_nat = natural_order(value_rows)
    padding = jnp.zeros((REACH, STRETCH, KVHEADS * HEAD_DIM), key_rows.dtype)
    key_pad = jnp.concatenate([padding, key_nat], axis=0)
    value_pad = jnp.concatenate([padding, value_nat], axis=0)
    group = QHEADS // KVHEADS
    scale = HEAD_DIM ** -0.5
    window = (REACH + 1) * STRETCH

    def one_stretch(stretch_id):
        query_block = lax.dynamic_index_in_dim(query_nat, stretch_id, 0, keepdims=False)
        query_block = query_block.astype(jnp.float32).reshape(STRETCH, KVHEADS, group, HEAD_DIM)
        key_block = lax.dynamic_slice_in_dim(key_pad, stretch_id, REACH + 1, 0)
        key_block = key_block.astype(jnp.float32).reshape(window, KVHEADS, HEAD_DIM)
        value_block = lax.dynamic_slice_in_dim(value_pad, stretch_id, REACH + 1, 0)
        value_block = value_block.astype(jnp.float32).reshape(window, KVHEADS, HEAD_DIM)
        query_pos = (stretch_id * STRETCH + jnp.arange(STRETCH, dtype=jnp.int32)).astype(jnp.int32)
        key_pos = ((stretch_id - REACH) * STRETCH + jnp.arange(window, dtype=jnp.int32)).astype(jnp.int32)
        query_doc = doc_of(query_pos, starts)
        key_doc = doc_of(key_pos, starts)
        allowed = (key_doc[None, :] == query_doc[:, None]) & (key_pos[None, :] <= query_pos[:, None]) & (key_pos[None, :] >= 0)
        scores = jnp.einsum('qgjd,kgd->gjqk', query_block, key_block) * scale
        scores = jnp.where(allowed[None, None], scores, -jnp.inf)
        row_max = jnp.max(scores, axis=-1, keepdims=True)
        raised = jnp.exp(scores - row_max)
        denominator = jnp.sum(raised, axis=-1, keepdims=True)
        weights = lax.optimization_barrier(raised.astype(jnp.bfloat16)).astype(jnp.float32)
        mixed_values = jnp.einsum('gjqk,kgd->gjqd', weights, value_block) / denominator
        mixed_values = jnp.transpose(mixed_values, (2, 0, 1, 3)).reshape(STRETCH, QHEADS * HEAD_DIM)
        return mixed_values.astype(jnp.bfloat16)

    results = lax.map(one_stretch, jnp.arange(2 * N_CTX, dtype=jnp.int32))
    lower = results[:N_CTX]
    upper = jnp.flip(results[N_CTX:], axis=0)
    stacked = jnp.stack([lower, upper], axis=1)
    return stacked.reshape(SEQ, QHEADS * HEAD_DIM)
```

```python
import functools
import jax
import jax.numpy as jnp
from jax import lax
from jax.experimental import pallas as pl
from jax.experimental.pallas import tpu as pltpu
from jax.sharding import PartitionSpec as P

HEAD_DIM = 128
REACH = 3
STRETCH = 256
LANES = 2
ROWS = 128
KEYS = REACH * STRETCH + ROWS
WINDOW = (REACH + 1) * STRETCH
SCALE = HEAD_DIM ** (-0.5)
LOG2E = 1.4426950408889634
GROUP = 8


def kv_pack_kernel(key_ref, value_ref, out_ref):
    width = key_ref.shape[1] // 4
    for dest in range(4):
        out_ref[dest, :, :width] = key_ref[:, dest * width : (dest + 1) * width]
        out_ref[dest, :, width:] = value_ref[:, dest * width : (dest + 1) * width]


def kv_pack(key_rows, value_rows):
    rows, width = key_rows.shape
    return pl.pallas_call(
        kv_pack_kernel,
        out_shape=jax.ShapeDtypeStruct((4, rows, width // 2), key_rows.dtype),
        name="kv_pack",
    )(key_rows, value_rows)


def query_pack_kernel(query_ref, *out_refs):
    at = 0
    for out_ref in out_refs:
        width = out_ref.shape[2]
        out_ref[0] = query_ref[:, at : at + width]
        at += width


def query_pack(queries, widths):
    rows, width = queries.shape
    return pl.pallas_call(
        query_pack_kernel,
        grid=(4,),
        in_specs=[pl.BlockSpec((rows, width // 4), lambda d: (0, d))],
        out_specs=[pl.BlockSpec((1, rows, w), lambda d: (d, 0, 0)) for w in widths],
        out_shape=[jax.ShapeDtypeStruct((4, rows, w), queries.dtype) for w in widths],
        name="query_pack",
    )(queries)


def load_windows(kv_head, kv_local, ctx, count, own, up, down, far, mate, keys, values, sems):
    odd = lax.rem(ctx, 2) == 1
    last = ctx == count - 1
    before_last = ctx == count - 2
    key_col = pl.ds(kv_head * HEAD_DIM, HEAD_DIM)
    value_col = pl.ds((kv_local + kv_head) * HEAD_DIM, HEAD_DIM)

    def pair(source, row, lane, slot):
        rows = pl.ds(row, STRETCH)
        place = pl.ds(slot * STRETCH, STRETCH)
        sem = sems.at[lane, slot]
        return (
            pltpu.make_async_copy(source.at[rows, key_col], keys.at[lane, place, :], sem),
            pltpu.make_async_copy(
                source.at[rows, value_col], values.at[lane, place, pl.ds(0, HEAD_DIM)], sem
            ),
        )

    def start(condition, source, row, lane, slot):
        @pl.when(condition)
        def _():
            for copy in pair(source, row, lane, slot):
                copy.start()

    for lane in range(LANES):
        for copy in pair(own, lane * STRETCH, lane, 3):
            copy.start()
    for copy in pair(up, 0, 0, 1):
        copy.start()
    even = jnp.logical_not(odd)
    plain = ctx < count - 2
    start(odd, mate, STRETCH, 0, 0)
    start(even, far, 0, 0, 0)
    start(odd, mate, 0, 0, 2)
    start(even, mate, STRETCH, 0, 2)
    start(jnp.logical_and(even, plain), mate, 2 * STRETCH, 1, 0)
    start(jnp.logical_and(odd, plain), far, 0, 1, 0)
    start(before_last, own, 0, 1, 0)
    start(last, up, 0, 1, 0)
    start(plain, down, 0, 1, 1)
    start(before_last, mate, 2 * STRETCH, 1, 1)
    start(last, mate, 0, 1, 1)
    start(even, mate, 0, 1, 2)
    start(jnp.logical_and(odd, plain), mate, 2 * STRETCH, 1, 2)
    start(last, own, 0, 1, 2)

    def wait(lane):
        for slot in range(REACH + 1):
            for copy in pair(own, 0, lane, slot):
                copy.wait()

    return wait


def attention_kernel(
    kv_head, kv_local, count,
    ctx_ref, starts_ref, query_ref, own, up, down, far, mate, *rest,
):
    out_ref, keys, values, sems = rest[-4:]
    step = pl.program_id(0)
    ctx = ctx_ref[0]
    lane = step // 2
    half = lax.rem(step, 2)

    @pl.when(step == 0)
    def _():
        wait = load_windows(
            kv_head, kv_local, ctx, count, own, up, down, far, mate, keys, values, sems
        )
        values[:, :, HEAD_DIM:] = jnp.ones((LANES, WINDOW, HEAD_DIM), values.dtype)
        wait(0)
        wait(1)

    stretch = jnp.where(lane == 0, ctx, 2 * count - 1 - ctx)
    first = stretch * STRETCH + half * ROWS
    row_pos = first + lax.broadcasted_iota(jnp.int32, (ROWS, 1), 0)
    starts = starts_ref[...]
    row_start = jnp.max(jnp.where(starts <= row_pos, starts, 0), axis=1, keepdims=True)
    key_pos = first - REACH * STRETCH + lax.broadcasted_iota(jnp.int32, (ROWS, KEYS), 1)
    allowed = (key_pos >= row_start) & (key_pos <= row_pos)
    bias = jnp.where(allowed, 0.0, -jnp.inf).astype(jnp.float32)
    window = pl.ds(pl.multiple_of(half * ROWS, ROWS), KEYS)
    key = keys[lane, window, :]
    value = values[lane, window, :]
    heads = query_ref.shape[1] // HEAD_DIM
    for head in range(heads):
        cols = slice(head * HEAD_DIM, (head + 1) * HEAD_DIM)
        scores = lax.dot_general(
            query_ref[:, cols], key, (((1,), (1,)), ((), ())), preferred_element_type=jnp.float32
        )
        scores = scores + bias
        top = jnp.max(scores, axis=1, keepdims=True)
        raised = jnp.exp2((scores - top) * (SCALE * LOG2E)).astype(jnp.bfloat16)
        mixed = jnp.dot(raised, value, preferred_element_type=jnp.float32)
        out_ref[:, cols] = (mixed[:, :HEAD_DIM] / mixed[:, HEAD_DIM:]).astype(out_ref.dtype)


def attention(kv_head, kv_local, count, ctx, starts, query, own, up, down, far, mate, partial):
    rows, width = query.shape
    blocks = rows // ROWS
    any_spec = pl.BlockSpec(memory_space=pl.ANY)
    operands = [ctx, starts, query, own, up, down, far, mate]
    in_specs = [
        pl.BlockSpec(memory_space=pltpu.SMEM),
        pl.BlockSpec(starts.shape, lambda i: (0, 0)),
        pl.BlockSpec((ROWS, width), lambda i: (i, 0)),
        any_spec, any_spec, any_spec, any_spec, any_spec,
    ]
    aliases = {}
    if partial is not None:
        aliases = {len(operands): 0}
        operands.append(partial)
        in_specs.append(any_spec)
    return pl.pallas_call(
        functools.partial(attention_kernel, kv_head, kv_local, count),
        grid=(blocks,),
        in_specs=in_specs,
        out_specs=pl.BlockSpec((ROWS, width), lambda i: (i, kv_head)),
        out_shape=jax.ShapeDtypeStruct((rows, kv_local * width), query.dtype),
        scratch_shapes=[
            pltpu.VMEM((LANES, WINDOW, HEAD_DIM), jnp.bfloat16),
            pltpu.VMEM((LANES, WINDOW, 2 * HEAD_DIM), jnp.bfloat16),
            pltpu.SemaphoreType.DMA((LANES, REACH + 1)),
        ],
        input_output_aliases=aliases,
        name="attention",
    )(*operands)


def body(queries, key_rows, value_rows, doc_lengths):
    count = lax.axis_size("ctx")
    ctx = lax.axis_index("ctx")
    odd = lax.rem(ctx, 2) == 1

    def swap(block):
        return lax.all_to_all(block, "head", split_axis=0, concat_axis=0, tiled=True)

    kv = swap(kv_pack(key_rows, value_rows)).reshape(LANES * STRETCH, -1)
    kv_local = kv.shape[1] // (2 * HEAD_DIM)
    width = queries.shape[1] // (4 * kv_local)
    packed = query_pack(queries, [width] * kv_local)
    query = [swap(part).reshape(LANES * STRETCH, width) for part in packed]

    lane0, lane1 = kv[:STRETCH], kv[STRETCH:]
    up = lax.ppermute(lane0, "ctx", [(i, i + 2) for i in range(count - 2)])
    down = lax.ppermute(lane1, "ctx", [(i + 2, i) for i in range(count - 2)])
    route = [(i, i + 3) for i in range(1, count - 3, 2)]
    route += [(i + 3, i) for i in range(1, count - 3, 2)]
    route += [(count - 1, count - 3)]
    far = lax.ppermute(jnp.where(odd, lane0, lane1), "ctx", route)
    passed = jnp.concatenate(
        [jnp.where(odd, lane1, lane0), up, jnp.where(ctx == count - 1, lane0, down)], axis=0
    )
    mate = lax.ppermute(passed, "ctx", [(i, i ^ 1) for i in range(count)])

    sizes = doc_lengths * 2
    starts = (jnp.cumsum(sizes) - sizes).reshape(1, -1)
    where = ctx.reshape(1)
    out = None
    for kv_head in range(kv_local):
        out = attention(
            kv_head, kv_local, count, where, starts, query[kv_head],
            kv, up, down, far, mate, out,
        )
    return out


def solution(mesh):
    placed = (P(("ctx", "head"), None), P(("ctx", "head"), None), P(("ctx", "head"), None), P())
    return jax.shard_map(
        body, mesh=mesh, in_specs=placed, out_specs=P("ctx", "head"), check_vma=False
    )
```

```python
import functools
import jax
import jax.numpy as jnp
from jax import lax
from jax.experimental import pallas as pl
from jax.experimental.pallas import tpu as pltpu
from jax.sharding import PartitionSpec as P

HEAD_DIM = 128
REACH = 3
STRETCH = 256
LANES = 2
HEADS = 4
ROWS = 128
KEYS = REACH * STRETCH + ROWS
WINDOW = (REACH + 1) * STRETCH
GROUP = 8
PADDED = HEAD_DIM + 16
EXPONENT_SCALE = HEAD_DIM ** (-0.5) * 1.4426950408889634
SMALL, LARGE = 2.0**-60, 2.0**110
VMEM_LIMIT = 24 << 20
VMEM_SPEC = pl.BlockSpec(memory_space=pltpu.VMEM)
ANY_SPEC = pl.BlockSpec(memory_space=pl.ANY)
SMEM_SPEC = pl.BlockSpec(memory_space=pltpu.SMEM)
PARAMS = pltpu.CompilerParams(vmem_limit_bytes=VMEM_LIMIT)


def kv_pack_kernel(key_ref, value_ref, out_ref):
    width = key_ref.shape[1] // HEADS
    for dest in range(HEADS):
        out_ref[dest, :, :width] = key_ref[:, dest * width : (dest + 1) * width]
        out_ref[dest, :, width:] = value_ref[:, dest * width : (dest + 1) * width]


def kv_pack(key_rows, value_rows):
    rows, width = key_rows.shape
    return pl.pallas_call(
        kv_pack_kernel,
        in_specs=[VMEM_SPEC, VMEM_SPEC],
        out_specs=VMEM_SPEC,
        out_shape=jax.ShapeDtypeStruct((HEADS, rows, 2 * width // HEADS), key_rows.dtype),
        compiler_params=PARAMS,
        name="kv_pack",
    )(key_rows, value_rows)


def query_pack_kernel(place_ref, query_ref, *refs):
    out_refs, sems = refs[:-1], refs[-1]
    width = query_ref.shape[1] // HEADS
    copies = []
    for at, (shift, out_ref) in enumerate(zip((1, 3, 2), out_refs)):
        col = pl.multiple_of(lax.rem(place_ref[1] + shift, HEADS) * width, width)
        copies.append(
            pltpu.make_async_copy(query_ref.at[:, pl.ds(col, width)], out_ref, sems.at[at])
        )
    for copy in copies:
        copy.start()
    for copy in copies:
        copy.wait()


def query_pack(place, queries):
    rows, width = queries.shape
    block = jax.ShapeDtypeStruct((rows, width // HEADS), queries.dtype)
    return pl.pallas_call(
        query_pack_kernel,
        in_specs=[SMEM_SPEC, ANY_SPEC],
        out_specs=[ANY_SPEC] * 3,
        out_shape=[block] * 3,
        scratch_shapes=[pltpu.SemaphoreType.DMA((3,))],
        compiler_params=PARAMS,
        name="query_pack",
    )(place, queries)


def load_windows(ctx, count, own, up, down, far, mate, keys, values, sems):
    odd = lax.rem(ctx, 2) == 1
    even = jnp.logical_not(odd)
    last = ctx == count - 1
    before_last = ctx == count - 2
    plain = ctx < count - 2
    width = keys.shape[2]

    def piece(kind, source, row, lane, slot):
        return pltpu.make_async_copy(
            source.at[pl.ds(row, STRETCH), pl.ds((1 - kind) * width, width)],
            (values, keys)[kind].at[lane, pl.ds(slot * STRETCH, STRETCH), :],
            sems.at[kind, lane, slot],
        )

    def start(condition, source, row, lane, slot):
        @pl.when(condition)
        def _():
            for kind in range(2):
                piece(kind, source, row, lane, slot).start()

    for lane in range(LANES):
        for kind in range(2):
            piece(kind, own, lane * STRETCH, lane, 3).start()
    for kind in range(2):
        piece(kind, up, 0, 0, 1).start()
    start(odd, mate, STRETCH, 0, 0)
    start(even, far, 0, 0, 0)
    start(odd, mate, 0, 0, 2)
    start(even, mate, STRETCH, 0, 2)
    start(jnp.logical_and(even, plain), mate, 2 * STRETCH, 1, 0)
    start(jnp.logical_and(odd, plain), far, 0, 1, 0)
    start(before_last, own, 0, 1, 0)
    start(last, up, 0, 1, 0)
    start(plain, down, 0, 1, 1)
    start(before_last, mate, 2 * STRETCH, 1, 1)
    start(last, mate, 0, 1, 1)
    start(even, mate, 0, 1, 2)
    start(jnp.logical_and(odd, plain), mate, 2 * STRETCH, 1, 2)
    start(last, own, 0, 1, 2)

    def wait(kind, lane):
        for slot in range(REACH + 1):
            piece(kind, own, 0, lane, slot).wait()

    return wait


def attend(block, ctx, count, lengths, query, keys, values_t, bias, out):
    lane = block // 2
    half = lax.rem(block, 2)
    stretch = jnp.where(lane == 0, ctx, 2 * count - 1 - ctx)
    first = stretch * STRETCH + half * ROWS
    docs = lengths.shape[1]
    earlier = lax.broadcasted_iota(jnp.int32, (docs, docs), 1) < lax.broadcasted_iota(
        jnp.int32, (docs, docs), 0
    )
    starts = 2 * jnp.sum(jnp.where(earlier, lengths, 0), axis=1, keepdims=True)
    row_pos = first + lax.broadcasted_iota(jnp.int32, (1, ROWS), 1)
    row_start = jnp.max(jnp.where(starts <= row_pos, starts, 0), axis=0, keepdims=True)
    key_pos = first - REACH * STRETCH + lax.broadcasted_iota(jnp.int32, (KEYS, ROWS), 0)
    allowed = (key_pos >= row_start) & (key_pos <= row_pos)
    bias[...] = jnp.where(allowed, 0.0, -jnp.inf).astype(jnp.float32)
    window = pl.ds(pl.multiple_of(half * ROWS, ROWS), KEYS)
    kv_local = keys.shape[2] // HEAD_DIM

    def part(kv_head, base, heads, raise_by):
        cols = [pl.ds(base + at * HEAD_DIM, HEAD_DIM) for at in range(heads)]
        stacked = jnp.concatenate([query[:, col] for col in cols], axis=0)
        key = keys[lane, window, kv_head * HEAD_DIM : (kv_head + 1) * HEAD_DIM]
        scores = lax.dot_general(
            key, stacked, (((1,), (1,)), ((), ())), preferred_element_type=jnp.float32
        )
        masks = jnp.concatenate([bias[...]] * heads, axis=1)
        weights = jnp.exp2(raise_by(scores, masks)).astype(jnp.bfloat16)
        mixed = jnp.dot(
            values_t[lane, kv_head, :, window], weights, preferred_element_type=jnp.float32
        )
        total = mixed[HEAD_DIM : HEAD_DIM + 1]
        result = (mixed[:HEAD_DIM] / total).astype(out.dtype)
        for at, col in enumerate(cols):
            out[:, col] = result[:, at * HEAD_DIM : (at + 1) * HEAD_DIM].T
        return jnp.where((total >= SMALL) & (total <= LARGE), 0, 1)

    outside = [
        part(kv_head, kv_head * GROUP * HEAD_DIM, GROUP, lambda s, m: s * EXPONENT_SCALE + m)
        for kv_head in range(kv_local)
    ]

    @pl.when(jnp.max(functools.reduce(jnp.maximum, outside)) > 0)
    def _():
        def shifted(scores, masks):
            scores = scores + masks
            return (scores - jnp.max(scores, axis=0, keepdims=True)) * EXPONENT_SCALE

        for kv_head in range(kv_local):

            @pl.loop(0, GROUP)
            def _(head):
                base = pl.multiple_of((kv_head * GROUP + head) * HEAD_DIM, HEAD_DIM)
                part(kv_head, base, 1, shifted)


def first_kernel(
    count, place_ref, lengths_ref, own, up, down, far, mate, queries, left, right,
    out_ref, keys, values_t, values, query, result, bias, sems, load_sems, store_sems,
):
    ctx, head = place_ref[0], place_ref[1]
    width = query.shape[2]
    wait = load_windows(ctx, count, own, up, down, far, mate, keys, values, sems)
    own_cols = pl.ds(pl.multiple_of(head * width, width), width)
    sources = (queries.at[:, own_cols], left, right)
    loads = [
        pltpu.make_async_copy(source, query.at[at], load_sems.at[at])
        for at, source in enumerate(sources)
    ]
    for load in loads:
        load.start()
    kv_local = keys.shape[2] // HEAD_DIM
    for lane in range(LANES):
        wait(0, lane)
        for kv_head in range(kv_local):
            values_t[lane, kv_head, :HEAD_DIM, :] = values[
                lane, :, kv_head * HEAD_DIM : (kv_head + 1) * HEAD_DIM
            ].T
            values_t[lane, kv_head, HEAD_DIM:, :] = jnp.ones(
                (PADDED - HEAD_DIM, WINDOW), values_t.dtype
            )
    for lane in range(LANES):
        wait(1, lane)
    for load in loads:
        load.wait()

    def store(at):
        shift = jnp.where(at == 0, 0, jnp.where(at == 1, 3, 1))
        block = lax.rem(head + shift, HEADS)
        rows = pl.ds(pl.multiple_of(block * ROWS, ROWS), ROWS)
        return block, pltpu.make_async_copy(result.at[at], out_ref.at[rows, :], store_sems.at[at])

    @pl.loop(0, 3)
    def _(at):
        block, copy = store(at)
        attend(
            block, ctx, count, lengths_ref[...], query.at[at], keys, values_t, bias, result.at[at]
        )
        copy.start()

    for at in range(3):
        store(at)[1].wait()


def last_kernel(
    count, place_ref, lengths_ref, query, keys, values_t, partial, out_ref, result, bias, sem
):
    ctx, head = place_ref[0], place_ref[1]
    block = lax.rem(head + 2, HEADS)
    attend(block, ctx, count, lengths_ref[...], query, keys, values_t, bias, result)
    rows = pl.ds(pl.multiple_of(block * ROWS, ROWS), ROWS)
    copy = pltpu.make_async_copy(result, out_ref.at[rows, :], sem)
    copy.start()
    copy.wait()


def attention(count, place, lengths, own, up, down, far, mate, queries, left, right, across):
    rows, width = left.shape
    kv_width = own.shape[1] // 2
    kv_local = kv_width // HEAD_DIM
    dtype = queries.dtype
    out_shape = jax.ShapeDtypeStruct((HEADS * rows, width), dtype)
    bias = pltpu.VMEM((KEYS, ROWS), jnp.float32)
    partial, keys, values_t = pl.pallas_call(
        functools.partial(first_kernel, count),
        in_specs=[SMEM_SPEC, VMEM_SPEC] + [VMEM_SPEC] * 5 + [ANY_SPEC] * 3,
        out_specs=[ANY_SPEC, VMEM_SPEC, VMEM_SPEC],
        out_shape=[
            out_shape,
            jax.ShapeDtypeStruct((LANES, WINDOW, kv_width), dtype),
            jax.ShapeDtypeStruct((LANES, kv_local, PADDED, WINDOW), dtype),
        ],
        scratch_shapes=[
            pltpu.VMEM((LANES, WINDOW, kv_width), dtype),
            pltpu.VMEM((3, rows, width), dtype),
            pltpu.VMEM((3, rows, width), dtype),
            bias,
            pltpu.SemaphoreType.DMA((2, LANES, REACH + 1)),
            pltpu.SemaphoreType.DMA((3,)),
            pltpu.SemaphoreType.DMA((3,)),
        ],
        compiler_params=PARAMS,
        name="attention_first",
    )(place, lengths, own, up, down, far, mate, queries, left, right)
    return pl.pallas_call(
        functools.partial(last_kernel, count),
        in_specs=[SMEM_SPEC] + [VMEM_SPEC] * 4 + [ANY_SPEC],
        out_specs=ANY_SPEC,
        out_shape=out_shape,
        scratch_shapes=[pltpu.VMEM((rows, width), dtype), bias, pltpu.SemaphoreType.DMA],
        input_output_aliases={5: 0},
        compiler_params=PARAMS,
        name="attention_last",
    )(place, lengths, across, keys, values_t, partial)


def body(queries, key_rows, value_rows, doc_lengths):
    count = lax.axis_size("ctx")
    ctx = lax.axis_index("ctx")
    odd = lax.rem(ctx, 2) == 1
    place = jnp.stack([ctx, lax.axis_index("head")])

    packed = kv_pack(key_rows, value_rows)
    to_next, to_previous, to_opposite = query_pack(place, queries)
    kv = lax.all_to_all(packed, "head", split_axis=0, concat_axis=0, tiled=True)
    kv = kv.reshape(LANES * STRETCH, -1)

    def rotate(block, shift):
        return lax.ppermute(block, "head", [(i, (i + shift) % HEADS) for i in range(HEADS)])

    kv, to_next, to_previous, to_opposite = lax.optimization_barrier((kv, to_next, to_previous, to_opposite))
    left = rotate(to_next, 1)
    right = rotate(to_previous, 3)
    across = rotate(to_opposite, 2)

    lane0, lane1 = kv[:STRETCH], kv[STRETCH:]
    up = lax.ppermute(lane0, "ctx", [(i, i + 2) for i in range(count - 2)])
    down = lax.ppermute(lane1, "ctx", [(i + 2, i) for i in range(count - 2)])
    route = [(i, i + 3) for i in range(1, count - 3, 2)]
    route += [(i + 3, i) for i in range(1, count - 3, 2)]
    route += [(count - 1, count - 3)]
    far = lax.ppermute(jnp.where(odd, lane0, lane1), "ctx", route)
    up, down, far, left, right = lax.optimization_barrier((up, down, far, left, right))
    passed = jnp.concatenate(
        [jnp.where(odd, lane1, lane0), up, jnp.where(ctx == count - 1, lane0, down)], axis=0
    )
    mate = lax.ppermute(passed, "ctx", [(i, i ^ 1) for i in range(count)])
    lengths = doc_lengths.reshape(1, -1)
    return attention(
        count, place, lengths, kv, up, down, far, mate, queries, left, right, across
    )


def solution(mesh):
    placed = (P(("ctx", "head"), None), P(("ctx", "head"), None), P(("ctx", "head"), None), P())
    return jax.shard_map(
        body, mesh=mesh, in_specs=placed, out_specs=P("ctx", "head"), check_vma=False
    )
```

```python
import functools
import jax
import jax.numpy as jnp
from jax import lax
from jax.experimental import pallas as pl
from jax.experimental.pallas import tpu as pltpu
from jax.sharding import PartitionSpec as P

HEAD_DIM = 128
REACH = 3
STRETCH = 256
LANES = 2
HEADS = 4
ROWS = 128
KEYS = REACH * STRETCH + ROWS
WINDOW = (REACH + 1) * STRETCH
GROUP = 8
PADDED = HEAD_DIM + 16
EXPONENT_SCALE = HEAD_DIM ** (-0.5) * 1.4426950408889634
SMALL, LARGE = 2.0**-60, 2.0**110
VMEM_LIMIT = 24 << 20
VMEM_SPEC = pl.BlockSpec(memory_space=pltpu.VMEM)
ANY_SPEC = pl.BlockSpec(memory_space=pl.ANY)
SMEM_SPEC = pl.BlockSpec(memory_space=pltpu.SMEM)
PARAMS = pltpu.CompilerParams(vmem_limit_bytes=VMEM_LIMIT)


def kv_pack_kernel(key_ref, value_ref, out_ref, sems):
    width = key_ref.shape[1] // HEADS
    copies = [
        pltpu.make_async_copy(
            source.at[:, pl.ds(dest * width, width)],
            out_ref.at[dest, :, pl.ds(kind * width, width)],
            sems.at[kind, dest],
        )
        for kind, source in enumerate((key_ref, value_ref))
        for dest in range(HEADS)
    ]
    for copy in copies:
        copy.start()
    for copy in copies:
        copy.wait()


def kv_pack(key_rows, value_rows):
    rows, width = key_rows.shape
    return pl.pallas_call(
        kv_pack_kernel,
        in_specs=[ANY_SPEC, ANY_SPEC],
        out_specs=ANY_SPEC,
        out_shape=jax.ShapeDtypeStruct((HEADS, rows, 2 * width // HEADS), key_rows.dtype),
        scratch_shapes=[pltpu.SemaphoreType.DMA((2, HEADS))],
        compiler_params=pltpu.CompilerParams(vmem_limit_bytes=60 << 20),
        name="kv_pack",
    )(key_rows, value_rows)


def query_pack_kernel(place_ref, lengths_ref, query_ref, *refs):
    out_refs, starts_ref, sems = refs[:-2], refs[-2], refs[-1]
    width = query_ref.shape[1] // HEADS
    copies = []
    for at, (shift, out_ref) in enumerate(zip((1, 3, 2), out_refs)):
        col = pl.multiple_of(lax.rem(place_ref[1] + shift, HEADS) * width, width)
        copies.append(
            pltpu.make_async_copy(query_ref.at[:, pl.ds(col, width)], out_ref, sems.at[at])
        )
    for copy in copies:
        copy.start()
    docs = lengths_ref.shape[1]
    earlier = lax.broadcasted_iota(jnp.int32, (docs, docs), 1) < lax.broadcasted_iota(
        jnp.int32, (docs, docs), 0
    )
    starts_ref[...] = 2 * jnp.sum(jnp.where(earlier, lengths_ref[...], 0), axis=1, keepdims=True)
    for copy in copies:
        copy.wait()


def query_pack(place, lengths, queries):
    rows, width = queries.shape
    block = jax.ShapeDtypeStruct((rows, width // HEADS), queries.dtype)
    return pl.pallas_call(
        query_pack_kernel,
        in_specs=[SMEM_SPEC, VMEM_SPEC, ANY_SPEC],
        out_specs=[VMEM_SPEC] * 4,
        out_shape=[block] * 3 + [jax.ShapeDtypeStruct((lengths.shape[1], 1), jnp.int32)],
        scratch_shapes=[pltpu.SemaphoreType.DMA((3,))],
        compiler_params=PARAMS,
        name="query_pack",
    )(place, lengths, queries)


def load_windows(ctx, count, own, up, down, far, mate, mate_own, keys, values, sems):
    odd = lax.rem(ctx, 2) == 1
    even = jnp.logical_not(odd)
    last = ctx == count - 1
    before_last = ctx == count - 2
    plain = ctx < count - 2
    width = keys.shape[2]

    def piece(kind, source, row, lane, slot):
        return pltpu.make_async_copy(
            source.at[pl.ds(row, STRETCH), pl.ds((1 - kind) * width, width)],
            (values, keys)[kind].at[lane, pl.ds(slot * STRETCH, STRETCH), :],
            sems.at[kind, lane, slot],
        )

    def start(condition, source, row, lane, slot):
        @pl.when(condition)
        def _():
            for kind in range(2):
                piece(kind, source, row, lane, slot).start()

    for lane in range(LANES):
        for kind in range(2):
            piece(kind, own, lane * STRETCH, lane, 3).start()
    for kind in range(2):
        piece(kind, up, 0, 0, 1).start()
    start(odd, mate, 0, 0, 0)
    start(even, far, 0, 0, 0)
    start(odd, mate_own, 0, 0, 2)
    start(even, mate, 0, 0, 2)
    start(jnp.logical_and(even, plain), mate, STRETCH, 1, 0)
    start(jnp.logical_and(odd, plain), far, 0, 1, 0)
    start(before_last, own, 0, 1, 0)
    start(last, up, 0, 1, 0)
    start(plain, down, 0, 1, 1)
    start(before_last, mate, STRETCH, 1, 1)
    start(last, mate_own, 0, 1, 1)
    start(even, mate_own, 0, 1, 2)
    start(jnp.logical_and(odd, plain), mate, STRETCH, 1, 2)
    start(last, own, 0, 1, 2)

    def wait(kind, lane):
        for slot in range(REACH + 1):
            piece(kind, own, 0, lane, slot).wait()

    return wait


def attend(block, ctx, count, starts, query, keys, values_t, bias, out):
    lane = block // 2
    half = lax.rem(block, 2)
    stretch = jnp.where(lane == 0, ctx, 2 * count - 1 - ctx)
    first = stretch * STRETCH + half * ROWS
    row_pos = first + lax.broadcasted_iota(jnp.int32, (1, ROWS), 1)
    row_start = jnp.max(jnp.where(starts <= row_pos, starts, 0), axis=0, keepdims=True)
    key_pos = first - REACH * STRETCH + lax.broadcasted_iota(jnp.int32, (KEYS, ROWS), 0)
    allowed = (key_pos >= row_start) & (key_pos <= row_pos)
    bias[...] = jnp.where(allowed, 0.0, -jnp.inf).astype(jnp.float32)
    window = pl.ds(pl.multiple_of(half * ROWS, ROWS), KEYS)
    kv_local = keys.shape[2] // HEAD_DIM

    def part(kv_head, base, heads, raise_by):
        cols = [pl.ds(base + at * HEAD_DIM, HEAD_DIM) for at in range(heads)]
        stacked = jnp.concatenate([query[:, col] for col in cols], axis=0)
        key = keys[lane, window, kv_head * HEAD_DIM : (kv_head + 1) * HEAD_DIM]
        scores = lax.dot_general(
            key, stacked, (((1,), (1,)), ((), ())), preferred_element_type=jnp.float32
        )
        masks = jnp.concatenate([bias[...]] * heads, axis=1)
        weights = jnp.exp2(raise_by(scores, masks)).astype(jnp.bfloat16)
        mixed = jnp.dot(
            values_t[lane, kv_head, :, window], weights, preferred_element_type=jnp.float32
        )
        total = mixed[HEAD_DIM : HEAD_DIM + 1]
        result = (mixed[:HEAD_DIM] / total).astype(out.dtype)
        for at, col in enumerate(cols):
            out[:, col] = result[:, at * HEAD_DIM : (at + 1) * HEAD_DIM].T
        return jnp.where((total >= SMALL) & (total <= LARGE), 0, 1)

    outside = [
        part(kv_head, kv_head * GROUP * HEAD_DIM, GROUP, lambda s, m: s * EXPONENT_SCALE + m)
        for kv_head in range(kv_local)
    ]

    @pl.when(jnp.max(functools.reduce(jnp.maximum, outside)) > 0)
    def _():
        def shifted(scores, masks):
            scores = scores + masks
            return (scores - jnp.max(scores, axis=0, keepdims=True)) * EXPONENT_SCALE

        for kv_head in range(kv_local):

            @pl.loop(0, GROUP)
            def _(head):
                base = pl.multiple_of((kv_head * GROUP + head) * HEAD_DIM, HEAD_DIM)
                part(kv_head, base, 1, shifted)


def first_kernel(
    count, place_ref, starts_ref, own, up, down, far, mate, mate_own, queries, left, right,
    out_ref, keys, values_t, values, query, result, bias, sems, load_sems, store_sems,
):
    ctx, head = place_ref[0], place_ref[1]
    width = query.shape[2]
    wait = load_windows(ctx, count, own, up, down, far, mate, mate_own, keys, values, sems)
    own_cols = pl.ds(pl.multiple_of(head * width, width), width)
    sources = (queries.at[:, own_cols], left, right)
    loads = [
        pltpu.make_async_copy(source, query.at[at], load_sems.at[at])
        for at, source in enumerate(sources)
    ]
    for load in loads:
        load.start()
    kv_local = keys.shape[2] // HEAD_DIM
    for lane in range(LANES):
        wait(0, lane)
        for kv_head in range(kv_local):
            values_t[lane, kv_head, :HEAD_DIM, :] = values[
                lane, :, kv_head * HEAD_DIM : (kv_head + 1) * HEAD_DIM
            ].T
            values_t[lane, kv_head, HEAD_DIM:, :] = jnp.ones(
                (PADDED - HEAD_DIM, WINDOW), values_t.dtype
            )
    for lane in range(LANES):
        wait(1, lane)
    for load in loads:
        load.wait()

    def store(at):
        shift = jnp.where(at == 0, 0, jnp.where(at == 1, 3, 1))
        block = lax.rem(head + shift, HEADS)
        rows = pl.ds(pl.multiple_of(block * ROWS, ROWS), ROWS)
        return block, pltpu.make_async_copy(result.at[at], out_ref.at[rows, :], store_sems.at[at])

    @pl.loop(0, 3)
    def _(at):
        block, copy = store(at)
        attend(
            block, ctx, count, starts_ref[...], query.at[at], keys, values_t, bias, result.at[at]
        )
        copy.start()

    for at in range(3):
        store(at)[1].wait()


def last_kernel(
    count, place_ref, starts_ref, query, keys, values_t, partial, out_ref, result, bias, sem
):
    ctx, head = place_ref[0], place_ref[1]
    block = lax.rem(head + 2, HEADS)
    attend(block, ctx, count, starts_ref[...], query, keys, values_t, bias, result)
    rows = pl.ds(pl.multiple_of(block * ROWS, ROWS), ROWS)
    copy = pltpu.make_async_copy(result, out_ref.at[rows, :], sem)
    copy.start()
    copy.wait()


def attention(count, place, starts, own, up, down, far, mate, mate_own, queries, left, right, across):
    rows, width = left.shape
    kv_width = own.shape[1] // 2
    kv_local = kv_width // HEAD_DIM
    dtype = queries.dtype
    out_shape = jax.ShapeDtypeStruct((HEADS * rows, width), dtype)
    bias = pltpu.VMEM((KEYS, ROWS), jnp.float32)
    partial, keys, values_t = pl.pallas_call(
        functools.partial(first_kernel, count),
        in_specs=[SMEM_SPEC, VMEM_SPEC] + [VMEM_SPEC] * 6 + [ANY_SPEC] * 3,
        out_specs=[ANY_SPEC, VMEM_SPEC, VMEM_SPEC],
        out_shape=[
            out_shape,
            jax.ShapeDtypeStruct((LANES, WINDOW, kv_width), dtype),
            jax.ShapeDtypeStruct((LANES, kv_local, PADDED, WINDOW), dtype),
        ],
        scratch_shapes=[
            pltpu.VMEM((LANES, WINDOW, kv_width), dtype),
            pltpu.VMEM((3, rows, width), dtype),
            pltpu.VMEM((3, rows, width), dtype),
            bias,
            pltpu.SemaphoreType.DMA((2, LANES, REACH + 1)),
            pltpu.SemaphoreType.DMA((3,)),
            pltpu.SemaphoreType.DMA((3,)),
        ],
        compiler_params=PARAMS,
        name="attention_first",
    )(place, starts, own, up, down, far, mate, mate_own, queries, left, right)
    return pl.pallas_call(
        functools.partial(last_kernel, count),
        in_specs=[SMEM_SPEC] + [VMEM_SPEC] * 4 + [ANY_SPEC],
        out_specs=ANY_SPEC,
        out_shape=out_shape,
        scratch_shapes=[pltpu.VMEM((rows, width), dtype), bias, pltpu.SemaphoreType.DMA],
        input_output_aliases={5: 0},
        compiler_params=PARAMS,
        name="attention_last",
    )(place, starts, across, keys, values_t, partial)


def body(queries, key_rows, value_rows, doc_lengths):
    count = lax.axis_size("ctx")
    ctx = lax.axis_index("ctx")
    odd = lax.rem(ctx, 2) == 1
    place = jnp.stack([ctx, lax.axis_index("head")])

    packed = kv_pack(key_rows, value_rows)
    to_next, to_previous, to_opposite, starts = query_pack(place, doc_lengths.reshape(1, -1), queries)
    kv = lax.all_to_all(packed, "head", split_axis=0, concat_axis=0, tiled=True)
    kv = kv.reshape(LANES * STRETCH, -1)

    def rotate(block, shift):
        return lax.ppermute(block, "head", [(i, (i + shift) % HEADS) for i in range(HEADS)])

    kv, starts = lax.optimization_barrier((kv, starts))
    left = rotate(to_next, 1)
    right = rotate(to_previous, 3)
    across = rotate(to_opposite, 2)

    lane0, lane1 = kv[:STRETCH], kv[STRETCH:]
    up = lax.ppermute(lane0, "ctx", [(i, i + 2) for i in range(count - 2)])
    down = lax.ppermute(lane1, "ctx", [(i + 2, i) for i in range(count - 2)])
    route = [(i, i + 3) for i in range(1, count - 3, 2)]
    route += [(i + 3, i) for i in range(1, count - 3, 2)]
    route += [(count - 1, count - 3)]
    far = lax.ppermute(jnp.where(odd, lane0, lane1), "ctx", route)
    up, down, far = lax.optimization_barrier((up, down, far))
    passed = jnp.concatenate([up, jnp.where(ctx == count - 1, lane0, down)], axis=0)
    swap = [(i, i ^ 1) for i in range(count)]
    mate = lax.ppermute(passed, "ctx", swap)
    inner, left, right = lax.optimization_barrier((jnp.where(odd, lane1, lane0), left, right))
    mate_own = lax.ppermute(inner, "ctx", swap)
    return attention(
        count, place, starts, kv, up, down, far, mate, mate_own, queries, left, right, across
    )


def solution(mesh):
    placed = (P(("ctx", "head"), None), P(("ctx", "head"), None), P(("ctx", "head"), None), P())
    return jax.shard_map(
        body, mesh=mesh, in_specs=placed, out_specs=P("ctx", "head"), check_vma=False
    )
```

```python
import functools
import jax
import jax.numpy as jnp
from jax import lax
from jax.experimental import pallas as pl
from jax.experimental.pallas import tpu as pltpu
from jax.sharding import PartitionSpec as P

HEAD_DIM = 128
REACH = 3
STRETCH = 256
LANES = 2
HEADS = 4
ROWS = 128
KEYS = REACH * STRETCH + ROWS
WINDOW = (REACH + 1) * STRETCH
GROUP = 8
PADDED = HEAD_DIM + 16
EXPONENT_SCALE = HEAD_DIM ** (-0.5) * 1.4426950408889634
SMALL, LARGE = 2.0**-60, 2.0**110
VMEM_LIMIT = 24 << 20
VMEM_SPEC = pl.BlockSpec(memory_space=pltpu.VMEM)
ANY_SPEC = pl.BlockSpec(memory_space=pl.ANY)
SMEM_SPEC = pl.BlockSpec(memory_space=pltpu.SMEM)
PARAMS = pltpu.CompilerParams(vmem_limit_bytes=VMEM_LIMIT)


def kv_pack_kernel(key_ref, value_ref, out_ref, stage, sems):
    width = key_ref.shape[1] // HEADS
    loads = [
        pltpu.make_async_copy(source, stage.at[kind], sems.at[kind, HEADS])
        for kind, source in enumerate((key_ref, value_ref))
    ]
    for load in loads:
        load.start()
    stores = []
    for kind, load in enumerate(loads):
        load.wait()
        for dest in range(HEADS):
            store = pltpu.make_async_copy(
                stage.at[kind, :, pl.ds(dest * width, width)],
                out_ref.at[dest, :, pl.ds(kind * width, width)],
                sems.at[kind, dest],
            )
            store.start()
            stores.append(store)
    for store in stores:
        store.wait()


def kv_pack(key_rows, value_rows):
    rows, width = key_rows.shape
    return pl.pallas_call(
        kv_pack_kernel,
        in_specs=[ANY_SPEC, ANY_SPEC],
        out_specs=ANY_SPEC,
        out_shape=jax.ShapeDtypeStruct((HEADS, rows, 2 * width // HEADS), key_rows.dtype),
        scratch_shapes=[
            pltpu.VMEM((2, rows, width), key_rows.dtype),
            pltpu.SemaphoreType.DMA((2, HEADS + 1)),
        ],
        compiler_params=pltpu.CompilerParams(vmem_limit_bytes=60 << 20),
        name="kv_pack",
    )(key_rows, value_rows)


def query_pack_kernel(place_ref, lengths_ref, query_ref, *refs):
    out_refs, starts_ref, sems = refs[:-2], refs[-2], refs[-1]
    width = query_ref.shape[1] // HEADS
    copies = []
    for at, (shift, out_ref) in enumerate(zip((1, 3, 2), out_refs)):
        col = pl.multiple_of(lax.rem(place_ref[1] + shift, HEADS) * width, width)
        copies.append(
            pltpu.make_async_copy(query_ref.at[:, pl.ds(col, width)], out_ref, sems.at[at])
        )
    for copy in copies:
        copy.start()
    docs = lengths_ref.shape[1]
    earlier = lax.broadcasted_iota(jnp.int32, (docs, docs), 1) < lax.broadcasted_iota(
        jnp.int32, (docs, docs), 0
    )
    starts_ref[...] = 2 * jnp.sum(jnp.where(earlier, lengths_ref[...], 0), axis=1, keepdims=True)
    for copy in copies:
        copy.wait()


def query_pack(place, lengths, queries):
    rows, width = queries.shape
    block = jax.ShapeDtypeStruct((rows, width // HEADS), queries.dtype)
    return pl.pallas_call(
        query_pack_kernel,
        in_specs=[SMEM_SPEC, VMEM_SPEC, ANY_SPEC],
        out_specs=[VMEM_SPEC] * 4,
        out_shape=[block] * 3 + [jax.ShapeDtypeStruct((lengths.shape[1], 1), jnp.int32)],
        scratch_shapes=[pltpu.SemaphoreType.DMA((3,))],
        compiler_params=PARAMS,
        name="query_pack",
    )(place, lengths, queries)


def load_windows(ctx, count, own, up, down, far, mate, keys, values, sems):
    odd = lax.rem(ctx, 2) == 1
    even = jnp.logical_not(odd)
    last = ctx == count - 1
    before_last = ctx == count - 2
    plain = ctx < count - 2
    width = keys.shape[2]

    def piece(kind, source, row, lane, slot):
        return pltpu.make_async_copy(
            source.at[pl.ds(row, STRETCH), pl.ds((1 - kind) * width, width)],
            (values, keys)[kind].at[lane, pl.ds(slot * STRETCH, STRETCH), :],
            sems.at[kind, lane, slot],
        )

    def start(condition, source, row, lane, slot):
        @pl.when(condition)
        def _():
            for kind in range(2):
                piece(kind, source, row, lane, slot).start()

    for lane in range(LANES):
        for kind in range(2):
            piece(kind, own, lane * STRETCH, lane, 3).start()
    for kind in range(2):
        piece(kind, up, 0, 0, 1).start()
    start(odd, mate, 0, 0, 0)
    start(even, far, 0, 0, 0)
    start(odd, mate, 2 * STRETCH, 0, 2)
    start(even, mate, 0, 0, 2)
    start(jnp.logical_and(even, plain), mate, STRETCH, 1, 0)
    start(jnp.logical_and(odd, plain), far, 0, 1, 0)
    start(before_last, own, 0, 1, 0)
    start(last, up, 0, 1, 0)
    start(plain, down, 0, 1, 1)
    start(before_last, mate, STRETCH, 1, 1)
    start(last, mate, 2 * STRETCH, 1, 1)
    start(even, mate, 2 * STRETCH, 1, 2)
    start(jnp.logical_and(odd, plain), mate, STRETCH, 1, 2)
    start(last, own, 0, 1, 2)

    def wait(kind, lane):
        for slot in range(REACH + 1):
            piece(kind, own, 0, lane, slot).wait()

    return wait


def attend(block, ctx, count, starts, query, keys, values_t, bias, out):
    lane = block // 2
    half = lax.rem(block, 2)
    stretch = jnp.where(lane == 0, ctx, 2 * count - 1 - ctx)
    first = stretch * STRETCH + half * ROWS
    row_pos = first + lax.broadcasted_iota(jnp.int32, (1, ROWS), 1)
    row_start = jnp.max(jnp.where(starts <= row_pos, starts, 0), axis=0, keepdims=True)
    key_pos = first - REACH * STRETCH + lax.broadcasted_iota(jnp.int32, (KEYS, ROWS), 0)
    allowed = (key_pos >= row_start) & (key_pos <= row_pos)
    bias[...] = jnp.where(allowed, 0.0, -jnp.inf).astype(jnp.float32)
    window = pl.ds(pl.multiple_of(half * ROWS, ROWS), KEYS)
    kv_local = keys.shape[2] // HEAD_DIM

    def part(kv_head, base, heads, raise_by):
        cols = [pl.ds(base + at * HEAD_DIM, HEAD_DIM) for at in range(heads)]
        stacked = jnp.concatenate([query[:, col] for col in cols], axis=0)
        key = keys[lane, window, kv_head * HEAD_DIM : (kv_head + 1) * HEAD_DIM]
        scores = lax.dot_general(
            key, stacked, (((1,), (1,)), ((), ())), preferred_element_type=jnp.float32
        )
        masks = jnp.concatenate([bias[...]] * heads, axis=1)
        weights = jnp.exp2(raise_by(scores, masks)).astype(jnp.bfloat16)
        mixed = jnp.dot(
            values_t[lane, kv_head, :, window], weights, preferred_element_type=jnp.float32
        )
        total = mixed[HEAD_DIM : HEAD_DIM + 1]
        result = (mixed[:HEAD_DIM] / total).astype(out.dtype)
        for at, col in enumerate(cols):
            out[:, col] = result[:, at * HEAD_DIM : (at + 1) * HEAD_DIM].T
        return jnp.where((total >= SMALL) & (total <= LARGE), 0, 1)

    outside = [
        part(kv_head, kv_head * GROUP * HEAD_DIM, GROUP, lambda s, m: s * EXPONENT_SCALE + m)
        for kv_head in range(kv_local)
    ]

    @pl.when(jnp.max(functools.reduce(jnp.maximum, outside)) > 0)
    def _():
        def shifted(scores, masks):
            scores = scores + masks
            return (scores - jnp.max(scores, axis=0, keepdims=True)) * EXPONENT_SCALE

        for kv_head in range(kv_local):

            @pl.loop(0, GROUP)
            def _(head):
                base = pl.multiple_of((kv_head * GROUP + head) * HEAD_DIM, HEAD_DIM)
                part(kv_head, base, 1, shifted)


def first_kernel(
    count, place_ref, starts_ref, own, up, down, far, mate, queries, left, right,
    out_ref, keys, values_t, values, query, result, bias, sems, load_sems, store_sems,
):
    ctx, head = place_ref[0], place_ref[1]
    width = query.shape[2]
    wait = load_windows(ctx, count, own, up, down, far, mate, keys, values, sems)
    own_cols = pl.ds(pl.multiple_of(head * width, width), width)
    sources = (queries.at[:, own_cols], left, right)
    loads = [
        pltpu.make_async_copy(source, query.at[at], load_sems.at[at])
        for at, source in enumerate(sources)
    ]
    for load in loads:
        load.start()
    kv_local = keys.shape[2] // HEAD_DIM
    for lane in range(LANES):
        wait(0, lane)
        for kv_head in range(kv_local):
            values_t[lane, kv_head, :HEAD_DIM, :] = values[
                lane, :, kv_head * HEAD_DIM : (kv_head + 1) * HEAD_DIM
            ].T
            values_t[lane, kv_head, HEAD_DIM:, :] = jnp.ones(
                (PADDED - HEAD_DIM, WINDOW), values_t.dtype
            )
    for lane in range(LANES):
        wait(1, lane)
    for load in loads:
        load.wait()

    def store(at):
        shift = jnp.where(at == 0, 0, jnp.where(at == 1, 3, 1))
        block = lax.rem(head + shift, HEADS)
        rows = pl.ds(pl.multiple_of(block * ROWS, ROWS), ROWS)
        return block, pltpu.make_async_copy(result.at[at], out_ref.at[rows, :], store_sems.at[at])

    @pl.loop(0, 3)
    def _(at):
        block, copy = store(at)
        attend(
            block, ctx, count, starts_ref[...], query.at[at], keys, values_t, bias, result.at[at]
        )
        copy.start()

    for at in range(3):
        store(at)[1].wait()


def last_kernel(
    count, place_ref, starts_ref, query, keys, values_t, partial, out_ref, result, bias, sem
):
    ctx, head = place_ref[0], place_ref[1]
    block = lax.rem(head + 2, HEADS)
    attend(block, ctx, count, starts_ref[...], query, keys, values_t, bias, result)
    rows = pl.ds(pl.multiple_of(block * ROWS, ROWS), ROWS)
    copy = pltpu.make_async_copy(result, out_ref.at[rows, :], sem)
    copy.start()
    copy.wait()


def attention(count, place, starts, own, up, down, far, mate, queries, left, right, across):
    rows, width = left.shape
    kv_width = own.shape[1] // 2
    kv_local = kv_width // HEAD_DIM
    dtype = queries.dtype
    out_shape = jax.ShapeDtypeStruct((HEADS * rows, width), dtype)
    bias = pltpu.VMEM((KEYS, ROWS), jnp.float32)
    partial, keys, values_t = pl.pallas_call(
        functools.partial(first_kernel, count),
        in_specs=[SMEM_SPEC, VMEM_SPEC] + [VMEM_SPEC] * 5 + [ANY_SPEC] * 3,
        out_specs=[ANY_SPEC, VMEM_SPEC, VMEM_SPEC],
        out_shape=[
            out_shape,
            jax.ShapeDtypeStruct((LANES, WINDOW, kv_width), dtype),
            jax.ShapeDtypeStruct((LANES, kv_local, PADDED, WINDOW), dtype),
        ],
        scratch_shapes=[
            pltpu.VMEM((LANES, WINDOW, kv_width), dtype),
            pltpu.VMEM((3, rows, width), dtype),
            pltpu.VMEM((3, rows, width), dtype),
            bias,
            pltpu.SemaphoreType.DMA((2, LANES, REACH + 1)),
            pltpu.SemaphoreType.DMA((3,)),
            pltpu.SemaphoreType.DMA((3,)),
        ],
        compiler_params=PARAMS,
        name="attention_first",
    )(place, starts, own, up, down, far, mate, queries, left, right)
    return pl.pallas_call(
        functools.partial(last_kernel, count),
        in_specs=[SMEM_SPEC] + [VMEM_SPEC] * 4 + [ANY_SPEC],
        out_specs=ANY_SPEC,
        out_shape=out_shape,
        scratch_shapes=[pltpu.VMEM((rows, width), dtype), bias, pltpu.SemaphoreType.DMA],
        input_output_aliases={5: 0},
        compiler_params=PARAMS,
        name="attention_last",
    )(place, starts, across, keys, values_t, partial)


def body(queries, key_rows, value_rows, doc_lengths):
    count = lax.axis_size("ctx")
    ctx = lax.axis_index("ctx")
    odd = lax.rem(ctx, 2) == 1
    place = jnp.stack([ctx, lax.axis_index("head")])

    packed = kv_pack(key_rows, value_rows)
    to_next, to_previous, to_opposite, starts = query_pack(place, doc_lengths.reshape(1, -1), queries)
    kv = lax.all_to_all(packed, "head", split_axis=0, concat_axis=0, tiled=True)
    kv = kv.reshape(LANES * STRETCH, -1)

    def rotate(block, shift):
        return lax.ppermute(block, "head", [(i, (i + shift) % HEADS) for i in range(HEADS)])

    kv, starts = lax.optimization_barrier((kv, starts))
    left = rotate(to_next, 1)
    right = rotate(to_previous, 3)
    across = rotate(to_opposite, 2)

    lane0, lane1 = kv[:STRETCH], kv[STRETCH:]
    up = lax.ppermute(lane0, "ctx", [(i, i + 2) for i in range(count - 2)])
    down = lax.ppermute(lane1, "ctx", [(i + 2, i) for i in range(count - 2)])
    route = [(i, i + 3) for i in range(1, count - 3, 2)]
    route += [(i + 3, i) for i in range(1, count - 3, 2)]
    route += [(count - 1, count - 3)]
    far = lax.ppermute(jnp.where(odd, lane0, lane1), "ctx", route)
    up, down, far, left, right = lax.optimization_barrier((up, down, far, left, right))
    passed = jnp.concatenate(
        [up, jnp.where(ctx == count - 1, lane0, down), jnp.where(odd, lane1, lane0)], axis=0
    )
    mate = lax.ppermute(passed, "ctx", [(i, i ^ 1) for i in range(count)])
    return attention(
        count, place, starts, kv, up, down, far, mate, queries, left, right, across
    )


def solution(mesh):
    placed = (P(("ctx", "head"), None), P(("ctx", "head"), None), P(("ctx", "head"), None), P())
    return jax.shard_map(
        body, mesh=mesh, in_specs=placed, out_specs=P("ctx", "head"), check_vma=False
    )
```

```python
import functools
import jax
import jax.numpy as jnp
from jax import lax
from jax.experimental import pallas as pl
from jax.experimental.pallas import tpu as pltpu
from jax.sharding import PartitionSpec as P

HEAD_DIM = 128
REACH = 3
STRETCH = 256
LANES = 2
HEADS = 4
ROWS = 128
KEYS = REACH * STRETCH + ROWS
WINDOW = (REACH + 1) * STRETCH
GROUP = 8
PADDED = HEAD_DIM + 16
EXPONENT_SCALE = HEAD_DIM ** (-0.5) * 1.4426950408889634
SMALL, LARGE = 2.0**-60, 2.0**110
VMEM_LIMIT = 24 << 20
VMEM_SPEC = pl.BlockSpec(memory_space=pltpu.VMEM)
ANY_SPEC = pl.BlockSpec(memory_space=pl.ANY)
SMEM_SPEC = pl.BlockSpec(memory_space=pltpu.SMEM)
PARAMS = pltpu.CompilerParams(vmem_limit_bytes=VMEM_LIMIT)


def kv_pack_kernel(key_ref, value_ref, out_ref, stage, sems):
    width = key_ref.shape[1] // HEADS
    loads = [
        pltpu.make_async_copy(source, stage.at[kind], sems.at[kind, HEADS])
        for kind, source in enumerate((key_ref, value_ref))
    ]
    for load in loads:
        load.start()
    stores = []
    for kind, load in enumerate(loads):
        load.wait()
        for dest in range(HEADS):
            store = pltpu.make_async_copy(
                stage.at[kind, :, pl.ds(dest * width, width)],
                out_ref.at[dest, :, pl.ds(kind * width, width)],
                sems.at[kind, dest],
            )
            store.start()
            stores.append(store)
    for store in stores:
        store.wait()


def kv_pack(key_rows, value_rows):
    rows, width = key_rows.shape
    return pl.pallas_call(
        kv_pack_kernel,
        in_specs=[ANY_SPEC, ANY_SPEC],
        out_specs=ANY_SPEC,
        out_shape=jax.ShapeDtypeStruct((HEADS, rows, 2 * width // HEADS), key_rows.dtype),
        scratch_shapes=[
            pltpu.VMEM((2, rows, width), key_rows.dtype),
            pltpu.SemaphoreType.DMA((2, HEADS + 1)),
        ],
        compiler_params=pltpu.CompilerParams(vmem_limit_bytes=60 << 20),
        name="kv_pack",
    )(key_rows, value_rows)


def query_pack_kernel(place_ref, lengths_ref, query_ref, *refs):
    out_refs, starts_ref, sems = refs[:-2], refs[-2], refs[-1]
    width = query_ref.shape[1] // HEADS
    copies = []
    for at, (shift, out_ref) in enumerate(zip((1, 3, 2), out_refs)):
        col = pl.multiple_of(lax.rem(place_ref[1] + shift, HEADS) * width, width)
        copies.append(
            pltpu.make_async_copy(query_ref.at[:, pl.ds(col, width)], out_ref, sems.at[at])
        )
    for copy in copies:
        copy.start()
    docs = lengths_ref.shape[1]
    earlier = lax.broadcasted_iota(jnp.int32, (docs, docs), 1) < lax.broadcasted_iota(
        jnp.int32, (docs, docs), 0
    )
    starts_ref[...] = 2 * jnp.sum(jnp.where(earlier, lengths_ref[...], 0), axis=1, keepdims=True)
    for copy in copies:
        copy.wait()


def query_pack(place, lengths, queries):
    rows, width = queries.shape
    block = jax.ShapeDtypeStruct((rows, width // HEADS), queries.dtype)
    return pl.pallas_call(
        query_pack_kernel,
        in_specs=[SMEM_SPEC, VMEM_SPEC, ANY_SPEC],
        out_specs=[VMEM_SPEC] * 4,
        out_shape=[block] * 3 + [jax.ShapeDtypeStruct((lengths.shape[1], 1), jnp.int32)],
        scratch_shapes=[pltpu.SemaphoreType.DMA((3,))],
        compiler_params=PARAMS,
        name="query_pack",
    )(place, lengths, queries)


def load_windows(ctx, count, own, up, down, far, inner, mate_up, mate_down, keys, values, sems):
    odd = lax.rem(ctx, 2) == 1
    even = jnp.logical_not(odd)
    last = ctx == count - 1
    before_last = ctx == count - 2
    plain = ctx < count - 2
    width = keys.shape[2]

    def piece(kind, source, row, lane, slot):
        return pltpu.make_async_copy(
            source.at[pl.ds(row, STRETCH), pl.ds((1 - kind) * width, width)],
            (values, keys)[kind].at[lane, pl.ds(slot * STRETCH, STRETCH), :],
            sems.at[kind, lane, slot],
        )

    def start(condition, source, row, lane, slot):
        @pl.when(condition)
        def _():
            for kind in range(2):
                piece(kind, source, row, lane, slot).start()

    for lane in range(LANES):
        for kind in range(2):
            piece(kind, own, lane * STRETCH, lane, 3).start()
    for kind in range(2):
        piece(kind, up, 0, 0, 1).start()
    start(odd, mate_up, 0, 0, 0)
    start(even, far, 0, 0, 0)
    start(odd, inner, 0, 0, 2)
    start(even, mate_up, 0, 0, 2)
    start(jnp.logical_and(even, plain), mate_down, 0, 1, 0)
    start(jnp.logical_and(odd, plain), far, 0, 1, 0)
    start(before_last, own, 0, 1, 0)
    start(last, up, 0, 1, 0)
    start(plain, down, 0, 1, 1)
    start(before_last, mate_down, 0, 1, 1)
    start(last, inner, 0, 1, 1)
    start(even, inner, 0, 1, 2)
    start(jnp.logical_and(odd, plain), mate_down, 0, 1, 2)
    start(last, own, 0, 1, 2)

    def wait(kind, lane):
        for slot in range(REACH + 1):
            piece(kind, own, 0, lane, slot).wait()

    return wait


def attend(block, ctx, count, starts, query, keys, values_t, bias, out):
    lane = block // 2
    half = lax.rem(block, 2)
    stretch = jnp.where(lane == 0, ctx, 2 * count - 1 - ctx)
    first = stretch * STRETCH + half * ROWS
    row_pos = first + lax.broadcasted_iota(jnp.int32, (1, ROWS), 1)
    row_start = jnp.max(jnp.where(starts <= row_pos, starts, 0), axis=0, keepdims=True)
    key_pos = first - REACH * STRETCH + lax.broadcasted_iota(jnp.int32, (KEYS, ROWS), 0)
    allowed = (key_pos >= row_start) & (key_pos <= row_pos)
    bias[...] = jnp.where(allowed, 0.0, -jnp.inf).astype(jnp.float32)
    window = pl.ds(pl.multiple_of(half * ROWS, ROWS), KEYS)
    kv_local = keys.shape[2] // HEAD_DIM

    def part(kv_head, base, heads, raise_by):
        cols = [pl.ds(base + at * HEAD_DIM, HEAD_DIM) for at in range(heads)]
        stacked = jnp.concatenate([query[:, col] for col in cols], axis=0)
        key = keys[lane, window, kv_head * HEAD_DIM : (kv_head + 1) * HEAD_DIM]
        scores = lax.dot_general(
            key, stacked, (((1,), (1,)), ((), ())), preferred_element_type=jnp.float32
        )
        masks = jnp.concatenate([bias[...]] * heads, axis=1)
        weights = jnp.exp2(raise_by(scores, masks)).astype(jnp.bfloat16)
        mixed = jnp.dot(
            values_t[lane, kv_head, :, window], weights, preferred_element_type=jnp.float32
        )
        total = mixed[HEAD_DIM : HEAD_DIM + 1]
        result = (mixed[:HEAD_DIM] / total).astype(out.dtype)
        for at, col in enumerate(cols):
            out[:, col] = result[:, at * HEAD_DIM : (at + 1) * HEAD_DIM].T
        return jnp.where((total >= SMALL) & (total <= LARGE), 0, 1)

    outside = [
        part(kv_head, kv_head * GROUP * HEAD_DIM, GROUP, lambda s, m: s * EXPONENT_SCALE + m)
        for kv_head in range(kv_local)
    ]

    @pl.when(jnp.max(functools.reduce(jnp.maximum, outside)) > 0)
    def _():
        def shifted(scores, masks):
            scores = scores + masks
            return (scores - jnp.max(scores, axis=0, keepdims=True)) * EXPONENT_SCALE

        for kv_head in range(kv_local):

            @pl.loop(0, GROUP)
            def _(head):
                base = pl.multiple_of((kv_head * GROUP + head) * HEAD_DIM, HEAD_DIM)
                part(kv_head, base, 1, shifted)


def first_kernel(
    count, place_ref, starts_ref, own, up, down, far, inner, mate_up, mate_down, queries, left, right,
    out_ref, keys, values_t, values, query, result, bias, sems, load_sems, store_sems,
):
    ctx, head = place_ref[0], place_ref[1]
    width = query.shape[2]
    wait = load_windows(ctx, count, own, up, down, far, inner, mate_up, mate_down, keys, values, sems)
    own_cols = pl.ds(pl.multiple_of(head * width, width), width)
    sources = (queries.at[:, own_cols], left, right)
    loads = [
        pltpu.make_async_copy(source, query.at[at], load_sems.at[at])
        for at, source in enumerate(sources)
    ]
    for load in loads:
        load.start()
    kv_local = keys.shape[2] // HEAD_DIM
    for lane in range(LANES):
        wait(0, lane)
        for kv_head in range(kv_local):
            values_t[lane, kv_head, :HEAD_DIM, :] = values[
                lane, :, kv_head * HEAD_DIM : (kv_head + 1) * HEAD_DIM
            ].T
            values_t[lane, kv_head, HEAD_DIM:, :] = jnp.ones(
                (PADDED - HEAD_DIM, WINDOW), values_t.dtype
            )
    for lane in range(LANES):
        wait(1, lane)
    for load in loads:
        load.wait()

    def store(at):
        shift = jnp.where(at == 0, 0, jnp.where(at == 1, 3, 1))
        block = lax.rem(head + shift, HEADS)
        rows = pl.ds(pl.multiple_of(block * ROWS, ROWS), ROWS)
        return block, pltpu.make_async_copy(result.at[at], out_ref.at[rows, :], store_sems.at[at])

    @pl.loop(0, 3)
    def _(at):
        block, copy = store(at)
        attend(
            block, ctx, count, starts_ref[...], query.at[at], keys, values_t, bias, result.at[at]
        )
        copy.start()

    for at in range(3):
        store(at)[1].wait()


def last_kernel(
    count, place_ref, starts_ref, query, keys, values_t, partial, out_ref, result, bias, sem
):
    ctx, head = place_ref[0], place_ref[1]
    block = lax.rem(head + 2, HEADS)
    attend(block, ctx, count, starts_ref[...], query, keys, values_t, bias, result)
    rows = pl.ds(pl.multiple_of(block * ROWS, ROWS), ROWS)
    copy = pltpu.make_async_copy(result, out_ref.at[rows, :], sem)
    copy.start()
    copy.wait()


def attention(count, place, starts, own, up, down, far, inner, mate_up, mate_down, queries, left, right, across):
    rows, width = left.shape
    kv_width = own.shape[1] // 2
    kv_local = kv_width // HEAD_DIM
    dtype = queries.dtype
    out_shape = jax.ShapeDtypeStruct((HEADS * rows, width), dtype)
    bias = pltpu.VMEM((KEYS, ROWS), jnp.float32)
    partial, keys, values_t = pl.pallas_call(
        functools.partial(first_kernel, count),
        in_specs=[SMEM_SPEC, VMEM_SPEC] + [VMEM_SPEC] * 7 + [ANY_SPEC] * 3,
        out_specs=[ANY_SPEC, VMEM_SPEC, VMEM_SPEC],
        out_shape=[
            out_shape,
            jax.ShapeDtypeStruct((LANES, WINDOW, kv_width), dtype),
            jax.ShapeDtypeStruct((LANES, kv_local, PADDED, WINDOW), dtype),
        ],
        scratch_shapes=[
            pltpu.VMEM((LANES, WINDOW, kv_width), dtype),
            pltpu.VMEM((3, rows, width), dtype),
            pltpu.VMEM((3, rows, width), dtype),
            bias,
            pltpu.SemaphoreType.DMA((2, LANES, REACH + 1)),
            pltpu.SemaphoreType.DMA((3,)),
            pltpu.SemaphoreType.DMA((3,)),
        ],
        compiler_params=PARAMS,
        name="attention_first",
    )(place, starts, own, up, down, far, inner, mate_up, mate_down, queries, left, right)
    return pl.pallas_call(
        functools.partial(last_kernel, count),
        in_specs=[SMEM_SPEC] + [VMEM_SPEC] * 4 + [ANY_SPEC],
        out_specs=ANY_SPEC,
        out_shape=out_shape,
        scratch_shapes=[pltpu.VMEM((rows, width), dtype), bias, pltpu.SemaphoreType.DMA],
        input_output_aliases={5: 0},
        compiler_params=PARAMS,
        name="attention_last",
    )(place, starts, across, keys, values_t, partial)


def body(queries, key_rows, value_rows, doc_lengths):
    count = lax.axis_size("ctx")
    ctx = lax.axis_index("ctx")
    odd = lax.rem(ctx, 2) == 1
    place = jnp.stack([ctx, lax.axis_index("head")])

    packed = kv_pack(key_rows, value_rows)
    to_next, to_previous, to_opposite, starts = query_pack(place, doc_lengths.reshape(1, -1), queries)
    kv = lax.all_to_all(packed, "head", split_axis=0, concat_axis=0, tiled=True)
    kv = kv.reshape(LANES * STRETCH, -1)

    def rotate(block, shift):
        return lax.ppermute(block, "head", [(i, (i + shift) % HEADS) for i in range(HEADS)])

    kv, starts = lax.optimization_barrier((kv, starts))
    left = rotate(to_next, 1)
    right = rotate(to_previous, 3)
    across = rotate(to_opposite, 2)

    lane0, lane1 = kv[:STRETCH], kv[STRETCH:]
    last = ctx == count - 1
    up = lax.ppermute(lane0, "ctx", [(i, i + 2) for i in range(count - 2)])
    down = lax.ppermute(lane1, "ctx", [(i + 2, i) for i in range(count - 2)])
    swap = [(i, i ^ 1) for i in range(count)]
    inner = lax.ppermute(jnp.where(odd, lane1, lane0), "ctx", swap)
    up, down, inner, left, right = lax.optimization_barrier((up, down, inner, left, right))
    above = jnp.where(last, lane0, down)
    mate_up = lax.ppermute(up, "ctx", swap)
    mate_down = lax.ppermute(above, "ctx", swap)
    route = [(i, i + 1) for i in range(1, count - 1, 2)]
    route += [(i, i - 1) for i in range(2, count - 2, 2)]
    route += [(count - 1, count - 3)]
    far = lax.ppermute(jnp.where(odd, jnp.where(last, lane0, up), above), "ctx", route)
    return attention(
        count, place, starts, kv, up, down, far, inner, mate_up, mate_down, queries, left, right, across
    )


def solution(mesh):
    placed = (P(("ctx", "head"), None), P(("ctx", "head"), None), P(("ctx", "head"), None), P())
    return jax.shard_map(
        body, mesh=mesh, in_specs=placed, out_specs=P("ctx", "head"), check_vma=False
    )
```

```python
import functools
import jax
import jax.numpy as jnp
from jax import lax
from jax.experimental import pallas as pl
from jax.experimental.pallas import tpu as pltpu
from jax.sharding import PartitionSpec as P

HEAD_DIM = 128
REACH = 3
STRETCH = 256
LANES = 2
HEADS = 4
ROWS = 128
KEYS = REACH * STRETCH + ROWS
WINDOW = (REACH + 1) * STRETCH
GROUP = 8
PADDED = HEAD_DIM + 16
EXPONENT_SCALE = HEAD_DIM ** (-0.5) * 1.4426950408889634
SMALL, LARGE = 2.0**-60, 2.0**110
VMEM_LIMIT = 24 << 20
VMEM_SPEC = pl.BlockSpec(memory_space=pltpu.VMEM)
ANY_SPEC = pl.BlockSpec(memory_space=pl.ANY)
SMEM_SPEC = pl.BlockSpec(memory_space=pltpu.SMEM)
PARAMS = pltpu.CompilerParams(vmem_limit_bytes=VMEM_LIMIT)


def kv_pack_kernel(key_ref, value_ref, out_ref, stage, sems):
    width = key_ref.shape[1] // HEADS
    loads = [
        pltpu.make_async_copy(source, stage.at[kind], sems.at[kind, HEADS])
        for kind, source in enumerate((key_ref, value_ref))
    ]
    for load in loads:
        load.start()
    stores = []
    for kind, load in enumerate(loads):
        load.wait()
        for dest in range(HEADS):
            store = pltpu.make_async_copy(
                stage.at[kind, :, pl.ds(dest * width, width)],
                out_ref.at[dest, :, pl.ds(kind * width, width)],
                sems.at[kind, dest],
            )
            store.start()
            stores.append(store)
    for store in stores:
        store.wait()


def kv_pack(key_rows, value_rows):
    rows, width = key_rows.shape
    return pl.pallas_call(
        kv_pack_kernel,
        in_specs=[ANY_SPEC, ANY_SPEC],
        out_specs=ANY_SPEC,
        out_shape=jax.ShapeDtypeStruct((HEADS, rows, 2 * width // HEADS), key_rows.dtype),
        scratch_shapes=[
            pltpu.VMEM((2, rows, width), key_rows.dtype),
            pltpu.SemaphoreType.DMA((2, HEADS + 1)),
        ],
        compiler_params=pltpu.CompilerParams(vmem_limit_bytes=60 << 20),
        name="kv_pack",
    )(key_rows, value_rows)


def query_pack_kernel(place_ref, lengths_ref, query_ref, *refs):
    out_refs, starts_ref, sems = refs[:-2], refs[-2], refs[-1]
    width = query_ref.shape[1] // HEADS
    copies = []
    for at, (shift, out_ref) in enumerate(zip((1, 3, 2), out_refs)):
        col = pl.multiple_of(lax.rem(place_ref[1] + shift, HEADS) * width, width)
        copies.append(
            pltpu.make_async_copy(query_ref.at[:, pl.ds(col, width)], out_ref, sems.at[at])
        )
    for copy in copies:
        copy.start()
    docs = lengths_ref.shape[1]
    earlier = lax.broadcasted_iota(jnp.int32, (docs, docs), 1) < lax.broadcasted_iota(
        jnp.int32, (docs, docs), 0
    )
    starts_ref[...] = 2 * jnp.sum(jnp.where(earlier, lengths_ref[...], 0), axis=1, keepdims=True)
    for copy in copies:
        copy.wait()


def query_pack(place, lengths, queries):
    rows, width = queries.shape
    block = jax.ShapeDtypeStruct((rows, width // HEADS), queries.dtype)
    return pl.pallas_call(
        query_pack_kernel,
        in_specs=[SMEM_SPEC, VMEM_SPEC, ANY_SPEC],
        out_specs=[VMEM_SPEC] * 4,
        out_shape=[block] * 3 + [jax.ShapeDtypeStruct((lengths.shape[1], 1), jnp.int32)],
        scratch_shapes=[pltpu.SemaphoreType.DMA((3,))],
        compiler_params=PARAMS,
        name="query_pack",
    )(place, lengths, queries)


def load_windows(ctx, count, own, up, down, far, inner, mate_up, mate_down, keys, values, sems):
    odd = lax.rem(ctx, 2) == 1
    even = jnp.logical_not(odd)
    last = ctx == count - 1
    before_last = ctx == count - 2
    plain = ctx < count - 2
    width = keys.shape[2]

    def piece(kind, source, row, lane, slot):
        return pltpu.make_async_copy(
            source.at[pl.ds(row, STRETCH), pl.ds((1 - kind) * width, width)],
            (values, keys)[kind].at[lane, pl.ds(slot * STRETCH, STRETCH), :],
            sems.at[kind, lane, slot],
        )

    def start(condition, source, row, lane, slot):
        @pl.when(condition)
        def _():
            for kind in range(2):
                piece(kind, source, row, lane, slot).start()

    for lane in range(LANES):
        for kind in range(2):
            piece(kind, own, lane * STRETCH, lane, 3).start()
    for kind in range(2):
        piece(kind, up, 0, 0, 1).start()
    start(odd, mate_up, 0, 0, 0)
    start(even, far, 0, 0, 0)
    start(odd, inner, 0, 0, 2)
    start(even, mate_up, 0, 0, 2)
    start(jnp.logical_and(even, plain), mate_down, 0, 1, 0)
    start(jnp.logical_and(odd, plain), far, 0, 1, 0)
    start(before_last, own, 0, 1, 0)
    start(last, up, 0, 1, 0)
    start(plain, down, 0, 1, 1)
    start(before_last, mate_down, 0, 1, 1)
    start(last, inner, 0, 1, 1)
    start(even, inner, 0, 1, 2)
    start(jnp.logical_and(odd, plain), mate_down, 0, 1, 2)
    start(last, own, 0, 1, 2)

    def wait(kind, lane):
        for slot in range(REACH + 1):
            piece(kind, own, 0, lane, slot).wait()

    return wait


def attend(block, ctx, count, starts, query, keys, values_t, bias, out):
    lane = block // 2
    half = lax.rem(block, 2)
    stretch = jnp.where(lane == 0, ctx, 2 * count - 1 - ctx)
    first = stretch * STRETCH + half * ROWS
    row_pos = first + lax.broadcasted_iota(jnp.int32, (1, ROWS), 1)
    row_start = jnp.max(jnp.where(starts <= row_pos, starts, 0), axis=0, keepdims=True)
    key_pos = first - REACH * STRETCH + lax.broadcasted_iota(jnp.int32, (KEYS, ROWS), 0)
    allowed = (key_pos >= row_start) & (key_pos <= row_pos)
    bias[...] = jnp.where(allowed, 0.0, -jnp.inf).astype(jnp.float32)
    window = pl.ds(pl.multiple_of(half * ROWS, ROWS), KEYS)
    kv_local = keys.shape[2] // HEAD_DIM

    def part(kv_head, base, heads, raise_by):
        cols = [pl.ds(base + at * HEAD_DIM, HEAD_DIM) for at in range(heads)]
        stacked = jnp.concatenate([query[:, col] for col in cols], axis=0)
        key = keys[lane, window, kv_head * HEAD_DIM : (kv_head + 1) * HEAD_DIM]
        scores = lax.dot_general(
            key, stacked, (((1,), (1,)), ((), ())), preferred_element_type=jnp.float32
        )
        masks = jnp.concatenate([bias[...]] * heads, axis=1)
        weights = jnp.exp2(raise_by(scores, masks)).astype(jnp.bfloat16)
        mixed = jnp.dot(
            values_t[lane, kv_head, :, window], weights, preferred_element_type=jnp.float32
        )
        total = mixed[HEAD_DIM : HEAD_DIM + 1]
        result = (mixed[:HEAD_DIM] / total).astype(out.dtype)
        for at, col in enumerate(cols):
            out[:, col] = result[:, at * HEAD_DIM : (at + 1) * HEAD_DIM].T
        return jnp.where((total >= SMALL) & (total <= LARGE), 0, 1)

    outside = [
        part(kv_head, kv_head * GROUP * HEAD_DIM, GROUP, lambda s, m: s * EXPONENT_SCALE + m)
        for kv_head in range(kv_local)
    ]

    @pl.when(jnp.max(functools.reduce(jnp.maximum, outside)) > 0)
    def _():
        def shifted(scores, masks):
            scores = scores + masks
            return (scores - jnp.max(scores, axis=0, keepdims=True)) * EXPONENT_SCALE

        for kv_head in range(kv_local):

            @pl.loop(0, GROUP)
            def _(head):
                base = pl.multiple_of((kv_head * GROUP + head) * HEAD_DIM, HEAD_DIM)
                part(kv_head, base, 1, shifted)


def first_kernel(
    count, place_ref, starts_ref, own, up, down, far, inner, mate_up, mate_down, queries, left, right,
    out_ref, keys, values_t, values, query, result, bias, sems, load_sems, store_sems,
):
    ctx, head = place_ref[0], place_ref[1]
    width = query.shape[2]
    wait = load_windows(ctx, count, own, up, down, far, inner, mate_up, mate_down, keys, values, sems)
    own_cols = pl.ds(pl.multiple_of(head * width, width), width)
    sources = (queries.at[:, own_cols], left, right)
    loads = [
        pltpu.make_async_copy(source, query.at[at], load_sems.at[at])
        for at, source in enumerate(sources)
    ]
    for load in loads:
        load.start()
    kv_local = keys.shape[2] // HEAD_DIM
    for lane in range(LANES):
        wait(0, lane)
        for kv_head in range(kv_local):
            values_t[lane, kv_head, :HEAD_DIM, :] = values[
                lane, :, kv_head * HEAD_DIM : (kv_head + 1) * HEAD_DIM
            ].T
            values_t[lane, kv_head, HEAD_DIM:, :] = jnp.ones(
                (PADDED - HEAD_DIM, WINDOW), values_t.dtype
            )
    for lane in range(LANES):
        wait(1, lane)
    for load in loads:
        load.wait()

    def store(at):
        shift = jnp.where(at == 0, 0, jnp.where(at == 1, 3, 1))
        block = lax.rem(head + shift, HEADS)
        rows = pl.ds(pl.multiple_of(block * ROWS, ROWS), ROWS)
        return block, pltpu.make_async_copy(result.at[at], out_ref.at[rows, :], store_sems.at[at])

    @pl.loop(0, 3)
    def _(at):
        block, copy = store(at)
        attend(
            block, ctx, count, starts_ref[...], query.at[at], keys, values_t, bias, result.at[at]
        )
        copy.start()

    for at in range(3):
        store(at)[1].wait()


def last_kernel(
    count, place_ref, starts_ref, query, keys, values_t, partial, out_ref, result, bias, sem
):
    ctx, head = place_ref[0], place_ref[1]
    block = lax.rem(head + 2, HEADS)
    attend(block, ctx, count, starts_ref[...], query, keys, values_t, bias, result)
    rows = pl.ds(pl.multiple_of(block * ROWS, ROWS), ROWS)
    copy = pltpu.make_async_copy(result, out_ref.at[rows, :], sem)
    copy.start()
    copy.wait()


def attention(count, place, starts, own, up, down, far, inner, mate_up, mate_down, queries, left, right, across):
    rows, width = left.shape
    kv_width = own.shape[1] // 2
    kv_local = kv_width // HEAD_DIM
    dtype = queries.dtype
    out_shape = jax.ShapeDtypeStruct((HEADS * rows, width), dtype)
    bias = pltpu.VMEM((KEYS, ROWS), jnp.float32)
    partial, keys, values_t = pl.pallas_call(
        functools.partial(first_kernel, count),
        in_specs=[SMEM_SPEC, VMEM_SPEC] + [VMEM_SPEC] * 7 + [ANY_SPEC] * 3,
        out_specs=[ANY_SPEC, VMEM_SPEC, VMEM_SPEC],
        out_shape=[
            out_shape,
            jax.ShapeDtypeStruct((LANES, WINDOW, kv_width), dtype),
            jax.ShapeDtypeStruct((LANES, kv_local, PADDED, WINDOW), dtype),
        ],
        scratch_shapes=[
            pltpu.VMEM((LANES, WINDOW, kv_width), dtype),
            pltpu.VMEM((3, rows, width), dtype),
            pltpu.VMEM((3, rows, width), dtype),
            bias,
            pltpu.SemaphoreType.DMA((2, LANES, REACH + 1)),
            pltpu.SemaphoreType.DMA((3,)),
            pltpu.SemaphoreType.DMA((3,)),
        ],
        compiler_params=PARAMS,
        name="attention_first",
    )(place, starts, own, up, down, far, inner, mate_up, mate_down, queries, left, right)
    return pl.pallas_call(
        functools.partial(last_kernel, count),
        in_specs=[SMEM_SPEC] + [VMEM_SPEC] * 4 + [ANY_SPEC],
        out_specs=ANY_SPEC,
        out_shape=out_shape,
        scratch_shapes=[pltpu.VMEM((rows, width), dtype), bias, pltpu.SemaphoreType.DMA],
        input_output_aliases={5: 0},
        compiler_params=PARAMS,
        name="attention_last",
    )(place, starts, across, keys, values_t, partial)


def body(queries, key_rows, value_rows, doc_lengths):
    count = lax.axis_size("ctx")
    ctx = lax.axis_index("ctx")
    odd = lax.rem(ctx, 2) == 1
    place = jnp.stack([ctx, lax.axis_index("head")])

    packed = kv_pack(key_rows, value_rows)
    to_next, to_previous, to_opposite, starts = query_pack(place, doc_lengths.reshape(1, -1), queries)
    kv = lax.all_to_all(packed, "head", split_axis=0, concat_axis=0, tiled=True)
    kv = kv.reshape(LANES * STRETCH, -1)

    def rotate(block, shift):
        return lax.ppermute(block, "head", [(i, (i + shift) % HEADS) for i in range(HEADS)])

    kv, starts = lax.optimization_barrier((kv, starts))
    left = rotate(to_next, 1)
    right = rotate(to_previous, 3)
    across = rotate(to_opposite, 2)

    lane0, lane1 = kv[:STRETCH], kv[STRETCH:]
    last = ctx == count - 1
    up = lax.ppermute(lane0, "ctx", [(i, i + 2) for i in range(count - 2)])
    down = lax.ppermute(lane1, "ctx", [(i + 2, i) for i in range(count - 2)])
    swap = [(i, i ^ 1) for i in range(count)]
    inner = lax.ppermute(jnp.where(odd, lane1, lane0), "ctx", swap)
    down, up, inner, left, right = lax.optimization_barrier((down, up, inner, left, right))
    above = jnp.where(last, lane0, down)
    mate_up = lax.ppermute(up, "ctx", swap)
    mate_down = lax.ppermute(above, "ctx", swap)
    route = [(i, i + 1) for i in range(1, count - 1, 2)]
    route += [(i, i - 1) for i in range(2, count - 2, 2)]
    route += [(count - 1, count - 3)]
    far = lax.ppermute(jnp.where(odd, jnp.where(last, lane0, up), above), "ctx", route)
    return attention(
        count, place, starts, kv, up, down, far, inner, mate_up, mate_down, queries, left, right, across
    )


def solution(mesh):
    placed = (P(("ctx", "head"), None), P(("ctx", "head"), None), P(("ctx", "head"), None), P())
    return jax.shard_map(
        body, mesh=mesh, in_specs=placed, out_specs=P("ctx", "head"), check_vma=False
    )
```

```python
import functools
import jax
import jax.numpy as jnp
from jax import lax
from jax.experimental import pallas as pl
from jax.experimental.pallas import tpu as pltpu
from jax.sharding import PartitionSpec as P

HEAD_DIM = 128
REACH = 3
STRETCH = 256
LANES = 2
HEADS = 4
ROWS = 128
KEYS = REACH * STRETCH + ROWS
WINDOW = (REACH + 1) * STRETCH
GROUP = 8
PADDED = HEAD_DIM + 16
EXPONENT_SCALE = HEAD_DIM ** (-0.5) * 1.4426950408889634
SMALL, LARGE = 2.0**-60, 2.0**110
VMEM_LIMIT = 24 << 20
VMEM_SPEC = pl.BlockSpec(memory_space=pltpu.VMEM)
ANY_SPEC = pl.BlockSpec(memory_space=pl.ANY)
SMEM_SPEC = pl.BlockSpec(memory_space=pltpu.SMEM)
PARAMS = pltpu.CompilerParams(vmem_limit_bytes=VMEM_LIMIT)


def kv_pack_kernel(key_ref, value_ref, out_ref, stage, sems):
    width = key_ref.shape[1] // HEADS
    loads = [
        pltpu.make_async_copy(source, stage.at[kind], sems.at[kind, HEADS])
        for kind, source in enumerate((key_ref, value_ref))
    ]
    for load in loads:
        load.start()
    stores = []
    for kind, load in enumerate(loads):
        load.wait()
        for dest in range(HEADS):
            store = pltpu.make_async_copy(
                stage.at[kind, :, pl.ds(dest * width, width)],
                out_ref.at[dest, :, pl.ds(kind * width, width)],
                sems.at[kind, dest],
            )
            store.start()
            stores.append(store)
    for store in stores:
        store.wait()


def kv_pack(key_rows, value_rows):
    rows, width = key_rows.shape
    return pl.pallas_call(
        kv_pack_kernel,
        in_specs=[ANY_SPEC, ANY_SPEC],
        out_specs=ANY_SPEC,
        out_shape=jax.ShapeDtypeStruct((HEADS, rows, 2 * width // HEADS), key_rows.dtype),
        scratch_shapes=[
            pltpu.VMEM((2, rows, width), key_rows.dtype),
            pltpu.SemaphoreType.DMA((2, HEADS + 1)),
        ],
        compiler_params=pltpu.CompilerParams(vmem_limit_bytes=60 << 20),
        name="kv_pack",
    )(key_rows, value_rows)


def query_pack_kernel(place_ref, lengths_ref, query_ref, *refs):
    out_refs, starts_ref, sems = refs[:-2], refs[-2], refs[-1]
    width = query_ref.shape[1] // HEADS
    copies = []
    for at, (shift, out_ref) in enumerate(zip((1, 3, 2), out_refs)):
        col = pl.multiple_of(lax.rem(place_ref[1] + shift, HEADS) * width, width)
        copies.append(
            pltpu.make_async_copy(query_ref.at[:, pl.ds(col, width)], out_ref, sems.at[at])
        )
    for copy in copies:
        copy.start()
    docs = lengths_ref.shape[1]
    earlier = lax.broadcasted_iota(jnp.int32, (docs, docs), 1) < lax.broadcasted_iota(
        jnp.int32, (docs, docs), 0
    )
    starts_ref[...] = 2 * jnp.sum(jnp.where(earlier, lengths_ref[...], 0), axis=1, keepdims=True)
    for copy in copies:
        copy.wait()


def query_pack(place, lengths, queries):
    rows, width = queries.shape
    block = jax.ShapeDtypeStruct((rows, width // HEADS), queries.dtype)
    return pl.pallas_call(
        query_pack_kernel,
        in_specs=[SMEM_SPEC, VMEM_SPEC, ANY_SPEC],
        out_specs=[VMEM_SPEC] * 4,
        out_shape=[block] * 3 + [jax.ShapeDtypeStruct((lengths.shape[1], 1), jnp.int32)],
        scratch_shapes=[pltpu.SemaphoreType.DMA((3,))],
        compiler_params=PARAMS,
        name="query_pack",
    )(place, lengths, queries)


def load_windows(ctx, count, own, up, down, far, inner, mate_up, mate_down, keys, values, sems):
    odd = lax.rem(ctx, 2) == 1
    even = jnp.logical_not(odd)
    last = ctx == count - 1
    before_last = ctx == count - 2
    plain = ctx < count - 2
    width = keys.shape[2]

    def piece(kind, source, row, lane, slot):
        return pltpu.make_async_copy(
            source.at[pl.ds(row, STRETCH), pl.ds((1 - kind) * width, width)],
            (values, keys)[kind].at[lane, pl.ds(slot * STRETCH, STRETCH), :],
            sems.at[kind, lane, slot],
        )

    def start(condition, source, row, lane, slot):
        @pl.when(condition)
        def _():
            for kind in range(2):
                piece(kind, source, row, lane, slot).start()

    for lane in range(LANES):
        for kind in range(2):
            piece(kind, own, lane * STRETCH, lane, 3).start()
    for kind in range(2):
        piece(kind, up, 0, 0, 1).start()
    start(odd, mate_up, 0, 0, 0)
    start(even, far, 0, 0, 0)
    start(odd, inner, 0, 0, 2)
    start(even, mate_up, 0, 0, 2)
    start(jnp.logical_and(even, plain), mate_down, 0, 1, 0)
    start(jnp.logical_and(odd, plain), far, 0, 1, 0)
    start(before_last, own, 0, 1, 0)
    start(last, up, 0, 1, 0)
    start(plain, down, 0, 1, 1)
    start(before_last, mate_down, 0, 1, 1)
    start(last, inner, 0, 1, 1)
    start(even, inner, 0, 1, 2)
    start(jnp.logical_and(odd, plain), mate_down, 0, 1, 2)
    start(last, own, 0, 1, 2)

    def wait(kind, lane):
        for slot in range(REACH + 1):
            piece(kind, own, 0, lane, slot).wait()

    return wait


def attend(block, ctx, count, starts, query, keys, values_t, bias, out):
    lane = block // 2
    half = lax.rem(block, 2)
    stretch = jnp.where(lane == 0, ctx, 2 * count - 1 - ctx)
    first = stretch * STRETCH + half * ROWS
    row_pos = first + lax.broadcasted_iota(jnp.int32, (1, ROWS), 1)
    row_start = jnp.max(jnp.where(starts <= row_pos, starts, 0), axis=0, keepdims=True)
    key_pos = first - REACH * STRETCH + lax.broadcasted_iota(jnp.int32, (KEYS, ROWS), 0)
    allowed = (key_pos >= row_start) & (key_pos <= row_pos)
    bias[...] = jnp.where(allowed, 0.0, -jnp.inf).astype(jnp.float32)
    window = pl.ds(pl.multiple_of(half * ROWS, ROWS), KEYS)
    kv_local = keys.shape[2] // HEAD_DIM

    def part(kv_head, base, heads, raise_by):
        cols = [pl.ds(base + at * HEAD_DIM, HEAD_DIM) for at in range(heads)]
        stacked = jnp.concatenate([query[:, col] for col in cols], axis=0)
        key = keys[lane, window, kv_head * HEAD_DIM : (kv_head + 1) * HEAD_DIM]
        scores = lax.dot_general(
            key, stacked, (((1,), (1,)), ((), ())), preferred_element_type=jnp.float32
        )
        masks = jnp.concatenate([bias[...]] * heads, axis=1)
        weights = jnp.exp2(raise_by(scores, masks)).astype(jnp.bfloat16)
        mixed = jnp.dot(
            values_t[lane, kv_head, :, window], weights, preferred_element_type=jnp.float32
        )
        total = mixed[HEAD_DIM : HEAD_DIM + 1]
        result = (mixed[:HEAD_DIM] / total).astype(out.dtype)
        for at, col in enumerate(cols):
            out[:, col] = result[:, at * HEAD_DIM : (at + 1) * HEAD_DIM].T
        return jnp.where((total >= SMALL) & (total <= LARGE), 0, 1)

    outside = [
        part(kv_head, kv_head * GROUP * HEAD_DIM, GROUP, lambda s, m: s * EXPONENT_SCALE + m)
        for kv_head in range(kv_local)
    ]

    @pl.when(jnp.max(functools.reduce(jnp.maximum, outside)) > 0)
    def _():
        def shifted(scores, masks):
            scores = scores + masks
            return (scores - jnp.max(scores, axis=0, keepdims=True)) * EXPONENT_SCALE

        for kv_head in range(kv_local):

            @pl.loop(0, GROUP)
            def _(head):
                base = pl.multiple_of((kv_head * GROUP + head) * HEAD_DIM, HEAD_DIM)
                part(kv_head, base, 1, shifted)


def first_kernel(
    count, place_ref, starts_ref, own, up, down, far, inner, mate_up, mate_down, queries, left, right,
    out_ref, keys, values_t, values, query, result, bias, sems, load_sems, store_sems,
):
    ctx, head = place_ref[0], place_ref[1]
    width = query.shape[2]
    wait = load_windows(ctx, count, own, up, down, far, inner, mate_up, mate_down, keys, values, sems)
    own_cols = pl.ds(pl.multiple_of(head * width, width), width)
    sources = (queries.at[:, own_cols], left, right)
    loads = [
        pltpu.make_async_copy(source, query.at[at], load_sems.at[at])
        for at, source in enumerate(sources)
    ]
    for load in loads:
        load.start()
    kv_local = keys.shape[2] // HEAD_DIM
    for lane in range(LANES):
        wait(0, lane)
        for kv_head in range(kv_local):
            values_t[lane, kv_head, :HEAD_DIM, :] = values[
                lane, :, kv_head * HEAD_DIM : (kv_head + 1) * HEAD_DIM
            ].T
            values_t[lane, kv_head, HEAD_DIM:, :] = jnp.ones(
                (PADDED - HEAD_DIM, WINDOW), values_t.dtype
            )
    for lane in range(LANES):
        wait(1, lane)
    for load in loads:
        load.wait()

    def store(at):
        shift = jnp.where(at == 0, 0, jnp.where(at == 1, 3, 1))
        block = lax.rem(head + shift, HEADS)
        rows = pl.ds(pl.multiple_of(block * ROWS, ROWS), ROWS)
        return block, pltpu.make_async_copy(result.at[at], out_ref.at[rows, :], store_sems.at[at])

    @pl.loop(0, 3)
    def _(at):
        block, copy = store(at)
        attend(
            block, ctx, count, starts_ref[...], query.at[at], keys, values_t, bias, result.at[at]
        )
        copy.start()

    for at in range(3):
        store(at)[1].wait()


def last_kernel(
    count, place_ref, starts_ref, query, keys, values_t, partial, out_ref, result, bias, sem
):
    ctx, head = place_ref[0], place_ref[1]
    block = lax.rem(head + 2, HEADS)
    attend(block, ctx, count, starts_ref[...], query, keys, values_t, bias, result)
    rows = pl.ds(pl.multiple_of(block * ROWS, ROWS), ROWS)
    copy = pltpu.make_async_copy(result, out_ref.at[rows, :], sem)
    copy.start()
    copy.wait()


def attention(count, place, starts, own, up, down, far, inner, mate_up, mate_down, queries, left, right, across):
    rows, width = left.shape
    kv_width = own.shape[1] // 2
    kv_local = kv_width // HEAD_DIM
    dtype = queries.dtype
    out_shape = jax.ShapeDtypeStruct((HEADS * rows, width), dtype)
    bias = pltpu.VMEM((KEYS, ROWS), jnp.float32)
    partial, keys, values_t = pl.pallas_call(
        functools.partial(first_kernel, count),
        in_specs=[SMEM_SPEC, VMEM_SPEC] + [VMEM_SPEC] * 7 + [ANY_SPEC] * 3,
        out_specs=[ANY_SPEC, VMEM_SPEC, VMEM_SPEC],
        out_shape=[
            out_shape,
            jax.ShapeDtypeStruct((LANES, WINDOW, kv_width), dtype),
            jax.ShapeDtypeStruct((LANES, kv_local, PADDED, WINDOW), dtype),
        ],
        scratch_shapes=[
            pltpu.VMEM((LANES, WINDOW, kv_width), dtype),
            pltpu.VMEM((3, rows, width), dtype),
            pltpu.VMEM((3, rows, width), dtype),
            bias,
            pltpu.SemaphoreType.DMA((2, LANES, REACH + 1)),
            pltpu.SemaphoreType.DMA((3,)),
            pltpu.SemaphoreType.DMA((3,)),
        ],
        compiler_params=PARAMS,
        name="attention_first",
    )(place, starts, own, up, down, far, inner, mate_up, mate_down, queries, left, right)
    return pl.pallas_call(
        functools.partial(last_kernel, count),
        in_specs=[SMEM_SPEC] + [VMEM_SPEC] * 4 + [ANY_SPEC],
        out_specs=ANY_SPEC,
        out_shape=out_shape,
        scratch_shapes=[pltpu.VMEM((rows, width), dtype), bias, pltpu.SemaphoreType.DMA],
        input_output_aliases={5: 0},
        compiler_params=PARAMS,
        name="attention_last",
    )(place, starts, across, keys, values_t, partial)


def body(queries, key_rows, value_rows, doc_lengths):
    count = lax.axis_size("ctx")
    ctx = lax.axis_index("ctx")
    odd = lax.rem(ctx, 2) == 1
    place = jnp.stack([ctx, lax.axis_index("head")])

    packed = kv_pack(key_rows, value_rows)
    to_next, to_previous, to_opposite, starts = query_pack(place, doc_lengths.reshape(1, -1), queries)
    kv = lax.all_to_all(packed, "head", split_axis=0, concat_axis=0, tiled=True)
    kv = kv.reshape(LANES * STRETCH, -1)

    def rotate(block, shift):
        return lax.ppermute(block, "head", [(i, (i + shift) % HEADS) for i in range(HEADS)])

    kv, starts = lax.optimization_barrier((kv, starts))
    left = rotate(to_next, 1)
    right = rotate(to_previous, 3)
    across = rotate(to_opposite, 2)

    lane0, lane1 = kv[:STRETCH], kv[STRETCH:]
    last = ctx == count - 1
    swap = [(i, i ^ 1) for i in range(count)]
    up = lax.ppermute(lane0, "ctx", [(i, i + 2) for i in range(count - 2)])
    down = lax.ppermute(lane1, "ctx", [(i + 2, i) for i in range(count - 2)])
    route = [(i, i + 3) for i in range(1, count - 3, 2)]
    route += [(i + 3, i) for i in range(1, count - 3, 2)]
    route += [(count - 1, count - 3)]
    far = lax.ppermute(jnp.where(odd, lane0, lane1), "ctx", route)
    inner = lax.ppermute(jnp.where(odd, lane1, lane0), "ctx", swap)
    inner, far, down, up, left, right = lax.optimization_barrier((inner, far, down, up, left, right))
    mate_up = lax.ppermute(up, "ctx", swap)
    mate_down = lax.ppermute(jnp.where(last, lane0, down), "ctx", swap)
    return attention(
        count, place, starts, kv, up, down, far, inner, mate_up, mate_down, queries, left, right, across
    )


def solution(mesh):
    placed = (P(("ctx", "head"), None), P(("ctx", "head"), None), P(("ctx", "head"), None), P())
    return jax.shard_map(
        body, mesh=mesh, in_specs=placed, out_specs=P("ctx", "head"), check_vma=False
    )
```

```python
import functools
import jax
import jax.numpy as jnp
from jax import lax
from jax.experimental import pallas as pl
from jax.experimental.pallas import tpu as pltpu
from jax.sharding import PartitionSpec as P

HEAD_DIM = 128
REACH = 3
STRETCH = 256
LANES = 2
HEADS = 4
ROWS = 128
KEYS = REACH * STRETCH + ROWS
WINDOW = (REACH + 1) * STRETCH
GROUP = 8
PADDED = HEAD_DIM + 16
EXPONENT_SCALE = HEAD_DIM ** (-0.5) * 1.4426950408889634
SMALL, LARGE = 2.0**-60, 2.0**110
VMEM_LIMIT = 24 << 20
VMEM_SPEC = pl.BlockSpec(memory_space=pltpu.VMEM)
ANY_SPEC = pl.BlockSpec(memory_space=pl.ANY)
SMEM_SPEC = pl.BlockSpec(memory_space=pltpu.SMEM)
PARAMS = pltpu.CompilerParams(vmem_limit_bytes=VMEM_LIMIT)


def kv_pack_kernel(key_ref, value_ref, out_ref, stage, sems):
    width = key_ref.shape[1] // HEADS
    loads = [
        pltpu.make_async_copy(source, stage.at[kind], sems.at[kind, HEADS])
        for kind, source in enumerate((key_ref, value_ref))
    ]
    for load in loads:
        load.start()
    stores = []
    for kind, load in enumerate(loads):
        load.wait()
        for dest in range(HEADS):
            store = pltpu.make_async_copy(
                stage.at[kind, :, pl.ds(dest * width, width)],
                out_ref.at[dest, :, pl.ds(kind * width, width)],
                sems.at[kind, dest],
            )
            store.start()
            stores.append(store)
    for store in stores:
        store.wait()


def kv_pack(key_rows, value_rows):
    rows, width = key_rows.shape
    return pl.pallas_call(
        kv_pack_kernel,
        in_specs=[ANY_SPEC, ANY_SPEC],
        out_specs=ANY_SPEC,
        out_shape=jax.ShapeDtypeStruct((HEADS, rows, 2 * width // HEADS), key_rows.dtype),
        scratch_shapes=[
            pltpu.VMEM((2, rows, width), key_rows.dtype),
            pltpu.SemaphoreType.DMA((2, HEADS + 1)),
        ],
        compiler_params=pltpu.CompilerParams(vmem_limit_bytes=60 << 20),
        name="kv_pack",
    )(key_rows, value_rows)


def query_pack_kernel(place_ref, lengths_ref, query_ref, *refs):
    out_refs, starts_ref, sems = refs[:-2], refs[-2], refs[-1]
    width = query_ref.shape[1] // HEADS
    copies = []
    for at, (shift, out_ref) in enumerate(zip((1, 3, 2), out_refs)):
        col = pl.multiple_of(lax.rem(place_ref[1] + shift, HEADS) * width, width)
        copies.append(
            pltpu.make_async_copy(query_ref.at[:, pl.ds(col, width)], out_ref, sems.at[at])
        )
    for copy in copies:
        copy.start()
    docs = lengths_ref.shape[1]
    earlier = lax.broadcasted_iota(jnp.int32, (docs, docs), 1) < lax.broadcasted_iota(
        jnp.int32, (docs, docs), 0
    )
    starts_ref[...] = 2 * jnp.sum(jnp.where(earlier, lengths_ref[...], 0), axis=1, keepdims=True)
    for copy in copies:
        copy.wait()


def query_pack(place, lengths, queries):
    rows, width = queries.shape
    block = jax.ShapeDtypeStruct((rows, width // HEADS), queries.dtype)
    return pl.pallas_call(
        query_pack_kernel,
        in_specs=[SMEM_SPEC, VMEM_SPEC, ANY_SPEC],
        out_specs=[VMEM_SPEC] * 4,
        out_shape=[block] * 3 + [jax.ShapeDtypeStruct((lengths.shape[1], 1), jnp.int32)],
        scratch_shapes=[pltpu.SemaphoreType.DMA((3,))],
        compiler_params=PARAMS,
        name="query_pack",
    )(place, lengths, queries)


def load_windows(ctx, count, own, up, down, far, inner, mate_up, mate_down, keys, values, sems):
    odd = lax.rem(ctx, 2) == 1
    even = jnp.logical_not(odd)
    last = ctx == count - 1
    before_last = ctx == count - 2
    plain = ctx < count - 2
    width = keys.shape[2]

    def piece(kind, source, row, lane, slot):
        return pltpu.make_async_copy(
            source.at[pl.ds(row, STRETCH), pl.ds((1 - kind) * width, width)],
            (values, keys)[kind].at[lane, pl.ds(slot * STRETCH, STRETCH), :],
            sems.at[kind, lane, slot],
        )

    def start(condition, source, row, lane, slot):
        @pl.when(condition)
        def _():
            for kind in range(2):
                piece(kind, source, row, lane, slot).start()

    for lane in range(LANES):
        for kind in range(2):
            piece(kind, own, lane * STRETCH, lane, 3).start()
    for kind in range(2):
        piece(kind, up, 0, 0, 1).start()
    start(odd, mate_up, 0, 0, 0)
    start(even, far, 0, 0, 0)
    start(odd, inner, 0, 0, 2)
    start(even, mate_up, 0, 0, 2)
    start(jnp.logical_and(even, plain), mate_down, 0, 1, 0)
    start(jnp.logical_and(odd, plain), far, 0, 1, 0)
    start(before_last, own, 0, 1, 0)
    start(last, up, 0, 1, 0)
    start(plain, down, 0, 1, 1)
    start(before_last, mate_down, 0, 1, 1)
    start(last, inner, 0, 1, 1)
    start(even, inner, 0, 1, 2)
    start(jnp.logical_and(odd, plain), mate_down, 0, 1, 2)
    start(last, own, 0, 1, 2)

    def wait(kind, lane):
        for slot in range(REACH + 1):
            piece(kind, own, 0, lane, slot).wait()

    return wait


def attention_kernel(
    count, place_ref, starts_ref, own, up, down, far, inner, mate_up, mate_down,
    queries, left, right, across,
    out_ref, keys, values, values_t, query, result, bias, flags, sems, load_sems, store_sems,
):
    ctx, head = place_ref[0], place_ref[1]
    width = query.shape[2]
    kv_local = keys.shape[2] // HEAD_DIM
    part_width = width // kv_local
    wait = load_windows(
        ctx, count, own, up, down, far, inner, mate_up, mate_down, keys, values, sems
    )

    def load(shift, source):
        block = lax.rem(head + HEADS - shift, HEADS)
        return pltpu.make_async_copy(source, query.at[block], load_sems.at[shift])

    own_cols = pl.ds(pl.multiple_of(head * width, width), width)
    loads = [
        load(shift, source)
        for shift, source in enumerate((queries.at[:, own_cols], left, across, right))
    ]
    for copy in loads:
        copy.start()
    flags[...] = jnp.zeros_like(flags)

    def store(block, kv_head):
        rows = pl.ds(pl.multiple_of(block * ROWS, ROWS), ROWS)
        cols = pl.ds(kv_head * part_width, part_width)
        return pltpu.make_async_copy(
            result.at[block, :, cols], out_ref.at[rows, cols], store_sems.at[block, kv_head]
        )

    def set_bias(block):
        lane, half = block // 2, lax.rem(block, 2)
        stretch = jnp.where(lane == 0, ctx, 2 * count - 1 - ctx)
        first = stretch * STRETCH + half * ROWS
        starts = starts_ref[...]
        row_pos = first + lax.broadcasted_iota(jnp.int32, (1, ROWS), 1)
        row_start = jnp.max(jnp.where(starts <= row_pos, starts, 0), axis=0, keepdims=True)
        key_pos = first - REACH * STRETCH + lax.broadcasted_iota(jnp.int32, (KEYS, ROWS), 0)
        allowed = (key_pos >= row_start) & (key_pos <= row_pos)
        bias[...] = jnp.where(allowed, 0.0, -jnp.inf).astype(jnp.float32)

    def part(block, kv_head, base, heads, raise_by):
        lane, half = block // 2, lax.rem(block, 2)
        window = pl.ds(pl.multiple_of(half * ROWS, ROWS), KEYS)
        cols = [pl.ds(base + at * HEAD_DIM, HEAD_DIM) for at in range(heads)]
        stacked = jnp.concatenate([query[block, :, col] for col in cols], axis=0)
        key = keys[lane, window, kv_head * HEAD_DIM : (kv_head + 1) * HEAD_DIM]
        scores = lax.dot_general(
            key, stacked, (((1,), (1,)), ((), ())), preferred_element_type=jnp.float32
        )
        masks = jnp.concatenate([bias[...]] * heads, axis=1)
        weights = jnp.exp2(raise_by(scores, masks)).astype(jnp.bfloat16)
        mixed = jnp.dot(
            values_t[lane, kv_head, :, window], weights, preferred_element_type=jnp.float32
        )
        total = mixed[HEAD_DIM : HEAD_DIM + 1]
        part_result = (mixed[:HEAD_DIM] / total).astype(out_ref.dtype)
        for at, col in enumerate(cols):
            result[block, :, col] = part_result[:, at * HEAD_DIM : (at + 1) * HEAD_DIM].T
        return total

    for lane in range(LANES):
        wait(0, lane)
        for kv_head in range(kv_local):
            values_t[lane, kv_head, :HEAD_DIM, :] = values[
                lane, :, kv_head * HEAD_DIM : (kv_head + 1) * HEAD_DIM
            ].T
            values_t[lane, kv_head, HEAD_DIM:, :] = jnp.ones(
                (PADDED - HEAD_DIM, WINDOW), values_t.dtype
            )
    for lane in range(LANES):
        wait(1, lane)
    for copy in loads:
        copy.wait()

    @pl.loop(0, HEADS)
    def _(block):
        set_bias(block)
        for kv_head in range(kv_local):
            total = part(
                block, kv_head, kv_head * part_width, GROUP,
                lambda scores, masks: scores * EXPONENT_SCALE + masks,
            )
            inside = (total >= SMALL) & (total <= LARGE)
            flags[...] = jnp.maximum(flags[...], jnp.where(inside, 0.0, 1.0))
            store(block, kv_head).start()

    for block in range(HEADS):
        for kv_head in range(kv_local):
            store(block, kv_head).wait()

    @pl.when(jnp.max(flags[...]) > 0)
    def _():
        def shifted(scores, masks):
            scores = scores + masks
            return (scores - jnp.max(scores, axis=0, keepdims=True)) * EXPONENT_SCALE

        @pl.loop(0, HEADS)
        def _(block):
            set_bias(block)
            for kv_head in range(kv_local):

                @pl.loop(0, GROUP)
                def _(head):
                    base = pl.multiple_of(kv_head * part_width + head * HEAD_DIM, HEAD_DIM)
                    part(block, kv_head, base, 1, shifted)

                copy = store(block, kv_head)
                copy.start()
                copy.wait()


def attention(
    count, place, starts, own, up, down, far, inner, mate_up, mate_down,
    queries, left, right, across,
):
    rows, width = left.shape
    kv_width = own.shape[1] // 2
    kv_local = kv_width // HEAD_DIM
    dtype = queries.dtype
    return pl.pallas_call(
        functools.partial(attention_kernel, count),
        in_specs=[SMEM_SPEC, VMEM_SPEC] + [VMEM_SPEC] * 7 + [ANY_SPEC] * 4,
        out_specs=ANY_SPEC,
        out_shape=jax.ShapeDtypeStruct((HEADS * rows, width), dtype),
        scratch_shapes=[
            pltpu.VMEM((LANES, WINDOW, kv_width), dtype),
            pltpu.VMEM((LANES, WINDOW, kv_width), dtype),
            pltpu.VMEM((LANES, kv_local, PADDED, WINDOW), dtype),
            pltpu.VMEM((HEADS, rows, width), dtype),
            pltpu.VMEM((HEADS, rows, width), dtype),
            pltpu.VMEM((KEYS, ROWS), jnp.float32),
            pltpu.VMEM((1, GROUP * ROWS), jnp.float32),
            pltpu.SemaphoreType.DMA((2, LANES, REACH + 1)),
            pltpu.SemaphoreType.DMA((HEADS,)),
            pltpu.SemaphoreType.DMA((HEADS, kv_local)),
        ],
        compiler_params=PARAMS,
        name="attention",
    )(
        place, starts, own, up, down, far, inner, mate_up, mate_down,
        queries, left, right, across,
    )


def body(queries, key_rows, value_rows, doc_lengths):
    count = lax.axis_size("ctx")
    ctx = lax.axis_index("ctx")
    odd = lax.rem(ctx, 2) == 1
    place = jnp.stack([ctx, lax.axis_index("head")])

    packed = kv_pack(key_rows, value_rows)
    to_next, to_previous, to_opposite, starts = query_pack(place, doc_lengths.reshape(1, -1), queries)
    kv = lax.all_to_all(packed, "head", split_axis=0, concat_axis=0, tiled=True)
    kv = kv.reshape(LANES * STRETCH, -1)

    def rotate(block, shift):
        return lax.ppermute(block, "head", [(i, (i + shift) % HEADS) for i in range(HEADS)])

    kv, starts = lax.optimization_barrier((kv, starts))
    left = rotate(to_next, 1)
    right = rotate(to_previous, 3)
    across = rotate(to_opposite, 2)

    lane0, lane1 = kv[:STRETCH], kv[STRETCH:]
    last = ctx == count - 1
    swap = [(i, i ^ 1) for i in range(count)]
    up = lax.ppermute(lane0, "ctx", [(i, i + 2) for i in range(count - 2)])
    down = lax.ppermute(lane1, "ctx", [(i + 2, i) for i in range(count - 2)])
    route = [(i, i + 3) for i in range(1, count - 3, 2)]
    route += [(i + 3, i) for i in range(1, count - 3, 2)]
    route += [(count - 1, count - 3)]
    far = lax.ppermute(jnp.where(odd, lane0, lane1), "ctx", route)
    inner = lax.ppermute(jnp.where(odd, lane1, lane0), "ctx", swap)
    down, far, up, left, right = lax.optimization_barrier((down, far, up, left, right))
    mate_up = lax.ppermute(up, "ctx", swap)
    mate_down = lax.ppermute(jnp.where(last, lane0, down), "ctx", swap)
    return attention(
        count, place, starts, kv, up, down, far, inner, mate_up, mate_down, queries, left, right, across
    )


def solution(mesh):
    placed = (P(("ctx", "head"), None), P(("ctx", "head"), None), P(("ctx", "head"), None), P())
    return jax.shard_map(
        body, mesh=mesh, in_specs=placed, out_specs=P("ctx", "head"), check_vma=False
    )
```

```python
import functools
import jax
import jax.numpy as jnp
from jax import lax
from jax.experimental import pallas as pl
from jax.experimental.pallas import tpu as pltpu
from jax.sharding import PartitionSpec as P

HEAD_DIM = 128
REACH = 3
STRETCH = 256
LANES = 2
HEADS = 4
ROWS = 128
KEYS = REACH * STRETCH + ROWS
WINDOW = (REACH + 1) * STRETCH
GROUP = 8
SKIPS = (512, 256, 0)
PADDED = HEAD_DIM + 16
EXPONENT_SCALE = HEAD_DIM ** (-0.5) * 1.4426950408889634
SMALL, LARGE = 2.0**-60, 2.0**110
VMEM_LIMIT = 24 << 20
VMEM_SPEC = pl.BlockSpec(memory_space=pltpu.VMEM)
ANY_SPEC = pl.BlockSpec(memory_space=pl.ANY)
SMEM_SPEC = pl.BlockSpec(memory_space=pltpu.SMEM)
PARAMS = pltpu.CompilerParams(vmem_limit_bytes=VMEM_LIMIT)


def kv_pack_kernel(key_ref, value_ref, out_ref, stage, sems):
    width = key_ref.shape[1] // HEADS
    loads = [
        pltpu.make_async_copy(source, stage.at[kind], sems.at[kind, HEADS])
        for kind, source in enumerate((key_ref, value_ref))
    ]
    for load in loads:
        load.start()
    stores = []
    for kind, load in enumerate(loads):
        load.wait()
        for dest in range(HEADS):
            store = pltpu.make_async_copy(
                stage.at[kind, :, pl.ds(dest * width, width)],
                out_ref.at[dest, :, pl.ds(kind * width, width)],
                sems.at[kind, dest],
            )
            store.start()
            stores.append(store)
    for store in stores:
        store.wait()


def kv_pack(key_rows, value_rows):
    rows, width = key_rows.shape
    return pl.pallas_call(
        kv_pack_kernel,
        in_specs=[ANY_SPEC, ANY_SPEC],
        out_specs=ANY_SPEC,
        out_shape=jax.ShapeDtypeStruct((HEADS, rows, 2 * width // HEADS), key_rows.dtype),
        scratch_shapes=[
            pltpu.VMEM((2, rows, width), key_rows.dtype),
            pltpu.SemaphoreType.DMA((2, HEADS + 1)),
        ],
        compiler_params=pltpu.CompilerParams(vmem_limit_bytes=60 << 20),
        name="kv_pack",
    )(key_rows, value_rows)


def query_pack_kernel(count, place_ref, lengths_ref, query_ref, *refs):
    out_refs, starts_ref, reach_ref, sems = refs[:-3], refs[-3], refs[-2], refs[-1]
    width = query_ref.shape[1] // HEADS
    copies = []
    for at, (shift, out_ref) in enumerate(zip((1, 3, 2), out_refs)):
        col = pl.multiple_of(lax.rem(place_ref[1] + shift, HEADS) * width, width)
        copies.append(
            pltpu.make_async_copy(query_ref.at[:, pl.ds(col, width)], out_ref, sems.at[at])
        )
    for copy in copies:
        copy.start()
    docs = lengths_ref.shape[1]
    earlier = lax.broadcasted_iota(jnp.int32, (docs, docs), 1) < lax.broadcasted_iota(
        jnp.int32, (docs, docs), 0
    )
    starts = 2 * jnp.sum(jnp.where(earlier, lengths_ref[...], 0), axis=1, keepdims=True)
    starts_ref[...] = starts
    ctx = place_ref[0]
    for block in range(HEADS):
        stretch = ctx if block < 2 else 2 * count - 1 - ctx
        first = stretch * STRETCH + block % 2 * ROWS
        reach_ref[block] = first - jnp.max(jnp.where(starts <= first, starts, 0))
    for copy in copies:
        copy.wait()


def query_pack(count, place, lengths, queries):
    rows, width = queries.shape
    block = jax.ShapeDtypeStruct((rows, width // HEADS), queries.dtype)
    return pl.pallas_call(
        functools.partial(query_pack_kernel, count),
        in_specs=[SMEM_SPEC, VMEM_SPEC, ANY_SPEC],
        out_specs=[VMEM_SPEC] * 4 + [SMEM_SPEC],
        out_shape=[block] * 3 + [
            jax.ShapeDtypeStruct((lengths.shape[1], 1), jnp.int32),
            jax.ShapeDtypeStruct((HEADS,), jnp.int32),
        ],
        scratch_shapes=[pltpu.SemaphoreType.DMA((3,))],
        compiler_params=PARAMS,
        name="query_pack",
    )(place, lengths, queries)


def load_windows(ctx, count, own, up, down, far, inner, mate_up, mate_down, keys, values, sems):
    odd = lax.rem(ctx, 2) == 1
    even = jnp.logical_not(odd)
    last = ctx == count - 1
    before_last = ctx == count - 2
    plain = ctx < count - 2
    width = keys.shape[2]

    def piece(kind, source, row, lane, slot):
        return pltpu.make_async_copy(
            source.at[pl.ds(row, STRETCH), pl.ds((1 - kind) * width, width)],
            (values, keys)[kind].at[lane, pl.ds(slot * STRETCH, STRETCH), :],
            sems.at[kind, lane, slot],
        )

    def start(condition, source, row, lane, slot):
        @pl.when(condition)
        def _():
            for kind in range(2):
                piece(kind, source, row, lane, slot).start()

    for lane in range(LANES):
        for kind in range(2):
            piece(kind, own, lane * STRETCH, lane, 3).start()
    for kind in range(2):
        piece(kind, up, 0, 0, 1).start()
    start(odd, mate_up, 0, 0, 0)
    start(even, far, 0, 0, 0)
    start(odd, inner, 0, 0, 2)
    start(even, mate_up, 0, 0, 2)
    start(jnp.logical_and(even, plain), mate_down, 0, 1, 0)
    start(jnp.logical_and(odd, plain), far, 0, 1, 0)
    start(before_last, own, 0, 1, 0)
    start(last, up, 0, 1, 0)
    start(plain, down, 0, 1, 1)
    start(before_last, mate_down, 0, 1, 1)
    start(last, inner, 0, 1, 1)
    start(even, inner, 0, 1, 2)
    start(jnp.logical_and(odd, plain), mate_down, 0, 1, 2)
    start(last, own, 0, 1, 2)

    def wait(kind, lane):
        for slot in range(REACH + 1):
            piece(kind, own, 0, lane, slot).wait()

    return wait


def attention_kernel(
    count, place_ref, starts_ref, reach_ref, own, up, down, far, inner, mate_up, mate_down,
    queries, left, right, across,
    out_ref, keys, values, values_t, query, result, bias, flags, sems, load_sems, store_sems,
):
    ctx, head = place_ref[0], place_ref[1]
    width = query.shape[2]
    kv_local = keys.shape[2] // HEAD_DIM
    part_width = width // kv_local
    wait = load_windows(
        ctx, count, own, up, down, far, inner, mate_up, mate_down, keys, values, sems
    )

    def load(shift, source):
        block = lax.rem(head + HEADS - shift, HEADS)
        return pltpu.make_async_copy(source, query.at[block], load_sems.at[shift])

    own_cols = pl.ds(pl.multiple_of(head * width, width), width)
    loads = [
        load(shift, source)
        for shift, source in enumerate((queries.at[:, own_cols], left, across, right))
    ]
    for copy in loads:
        copy.start()
    flags[...] = jnp.zeros_like(flags)

    def store(block, kv_head):
        rows = pl.ds(pl.multiple_of(block * ROWS, ROWS), ROWS)
        cols = pl.ds(kv_head * part_width, part_width)
        return pltpu.make_async_copy(
            result.at[block, :, cols], out_ref.at[rows, cols], store_sems.at[block, kv_head]
        )

    def set_bias(block):
        lane, half = block // 2, lax.rem(block, 2)
        stretch = jnp.where(lane == 0, ctx, 2 * count - 1 - ctx)
        first = stretch * STRETCH + half * ROWS
        starts = starts_ref[...]
        row_pos = first + lax.broadcasted_iota(jnp.int32, (1, ROWS), 1)
        row_start = jnp.max(jnp.where(starts <= row_pos, starts, 0), axis=0, keepdims=True)
        key_pos = first - REACH * STRETCH + lax.broadcasted_iota(jnp.int32, (KEYS, ROWS), 0)
        allowed = (key_pos >= row_start) & (key_pos <= row_pos)
        bias[...] = jnp.where(allowed, 0.0, -jnp.inf).astype(jnp.float32)

    def part(block, kv_head, base, heads, raise_by, skip=0):
        lane, half = block // 2, lax.rem(block, 2)
        window = pl.ds(pl.multiple_of(half * ROWS + skip, ROWS), KEYS - skip)
        cols = [pl.ds(base + at * HEAD_DIM, HEAD_DIM) for at in range(heads)]
        stacked = jnp.concatenate([query[block, :, col] for col in cols], axis=0)
        key = keys[lane, window, kv_head * HEAD_DIM : (kv_head + 1) * HEAD_DIM]
        scores = lax.dot_general(
            key, stacked, (((1,), (1,)), ((), ())), preferred_element_type=jnp.float32
        )
        masks = jnp.concatenate([bias[skip:]] * heads, axis=1)
        weights = jnp.exp2(raise_by(scores, masks)).astype(jnp.bfloat16)
        mixed = jnp.dot(
            values_t[lane, kv_head, :, window], weights, preferred_element_type=jnp.float32
        )
        total = mixed[HEAD_DIM : HEAD_DIM + 1]
        part_result = (mixed[:HEAD_DIM] / total).astype(out_ref.dtype)
        for at, col in enumerate(cols):
            result[block, :, col] = part_result[:, at * HEAD_DIM : (at + 1) * HEAD_DIM].T
        return total

    for lane in range(LANES):
        wait(0, lane)
        for kv_head in range(kv_local):
            values_t[lane, kv_head, :HEAD_DIM, :] = values[
                lane, :, kv_head * HEAD_DIM : (kv_head + 1) * HEAD_DIM
            ].T
            values_t[lane, kv_head, HEAD_DIM:, :] = jnp.ones(
                (PADDED - HEAD_DIM, WINDOW), values_t.dtype
            )
    for lane in range(LANES):
        wait(1, lane)
    for copy in loads:
        copy.wait()

    @pl.loop(0, HEADS)
    def _(block):
        set_bias(block)
        reach = reach_ref[block]

        def run(skip, condition):
            @pl.when(condition)
            def _():
                for kv_head in range(kv_local):
                    total = part(
                        block, kv_head, kv_head * part_width, GROUP,
                        lambda scores, masks: scores * EXPONENT_SCALE + masks, skip,
                    )
                    inside = (total >= SMALL) & (total <= LARGE)
                    flags[...] = jnp.maximum(flags[...], jnp.where(inside, 0.0, 1.0))
                    store(block, kv_head).start()

        room = REACH * STRETCH
        low = 0
        for skip in SKIPS:
            run(skip, (reach > low) & (reach <= room - skip) if low else reach <= room - skip)
            low = room - skip

    for block in range(HEADS):
        for kv_head in range(kv_local):
            store(block, kv_head).wait()

    @pl.when(jnp.max(flags[...]) > 0)
    def _():
        def shifted(scores, masks):
            scores = scores + masks
            return (scores - jnp.max(scores, axis=0, keepdims=True)) * EXPONENT_SCALE

        @pl.loop(0, HEADS)
        def _(block):
            set_bias(block)
            for kv_head in range(kv_local):

                @pl.loop(0, GROUP)
                def _(head):
                    base = pl.multiple_of(kv_head * part_width + head * HEAD_DIM, HEAD_DIM)
                    part(block, kv_head, base, 1, shifted)

                copy = store(block, kv_head)
                copy.start()
                copy.wait()


def attention(
    count, place, starts, reach, own, up, down, far, inner, mate_up, mate_down,
    queries, left, right, across,
):
    rows, width = left.shape
    kv_width = own.shape[1] // 2
    kv_local = kv_width // HEAD_DIM
    dtype = queries.dtype
    return pl.pallas_call(
        functools.partial(attention_kernel, count),
        in_specs=[SMEM_SPEC, VMEM_SPEC, SMEM_SPEC] + [VMEM_SPEC] * 7 + [ANY_SPEC] * 4,
        out_specs=ANY_SPEC,
        out_shape=jax.ShapeDtypeStruct((HEADS * rows, width), dtype),
        scratch_shapes=[
            pltpu.VMEM((LANES, WINDOW, kv_width), dtype),
            pltpu.VMEM((LANES, WINDOW, kv_width), dtype),
            pltpu.VMEM((LANES, kv_local, PADDED, WINDOW), dtype),
            pltpu.VMEM((HEADS, rows, width), dtype),
            pltpu.VMEM((HEADS, rows, width), dtype),
            pltpu.VMEM((KEYS, ROWS), jnp.float32),
            pltpu.VMEM((1, GROUP * ROWS), jnp.float32),
            pltpu.SemaphoreType.DMA((2, LANES, REACH + 1)),
            pltpu.SemaphoreType.DMA((HEADS,)),
            pltpu.SemaphoreType.DMA((HEADS, kv_local)),
        ],
        compiler_params=PARAMS,
        name="attention",
    )(
        place, starts, reach, own, up, down, far, inner, mate_up, mate_down,
        queries, left, right, across,
    )


def body(queries, key_rows, value_rows, doc_lengths):
    count = lax.axis_size("ctx")
    ctx = lax.axis_index("ctx")
    odd = lax.rem(ctx, 2) == 1
    place = jnp.stack([ctx, lax.axis_index("head")])

    packed = kv_pack(key_rows, value_rows)
    to_next, to_previous, to_opposite, starts, reach = query_pack(count, place, doc_lengths.reshape(1, -1), queries)
    kv = lax.all_to_all(packed, "head", split_axis=0, concat_axis=0, tiled=True)
    kv = kv.reshape(LANES * STRETCH, -1)

    def rotate(block, shift):
        return lax.ppermute(block, "head", [(i, (i + shift) % HEADS) for i in range(HEADS)])

    kv, starts = lax.optimization_barrier((kv, starts))
    left = rotate(to_next, 1)
    right = rotate(to_previous, 3)
    across = rotate(to_opposite, 2)

    lane0, lane1 = kv[:STRETCH], kv[STRETCH:]
    last = ctx == count - 1
    swap = [(i, i ^ 1) for i in range(count)]
    up = lax.ppermute(lane0, "ctx", [(i, i + 2) for i in range(count - 2)])
    down = lax.ppermute(lane1, "ctx", [(i + 2, i) for i in range(count - 2)])
    route = [(i, i + 3) for i in range(1, count - 3, 2)]
    route += [(i + 3, i) for i in range(1, count - 3, 2)]
    route += [(count - 1, count - 3)]
    far = lax.ppermute(jnp.where(odd, lane0, lane1), "ctx", route)
    inner = lax.ppermute(jnp.where(odd, lane1, lane0), "ctx", swap)
    down, far, up, left, right = lax.optimization_barrier((down, far, up, left, right))
    mate_up = lax.ppermute(up, "ctx", swap)
    mate_down = lax.ppermute(jnp.where(last, lane0, down), "ctx", swap)
    return attention(
        count, place, starts, reach, kv, up, down, far, inner, mate_up, mate_down, queries, left, right, across
    )


def solution(mesh):
    placed = (P(("ctx", "head"), None), P(("ctx", "head"), None), P(("ctx", "head"), None), P())
    return jax.shard_map(
        body, mesh=mesh, in_specs=placed, out_specs=P("ctx", "head"), check_vma=False
    )
```

```python
import functools
import jax
import jax.numpy as jnp
from jax import lax
from jax.experimental import pallas as pl
from jax.experimental.pallas import tpu as pltpu
from jax.sharding import PartitionSpec as P

HEAD_DIM = 128
REACH = 3
STRETCH = 256
LANES = 2
HEADS = 4
ROWS = 128
KEYS = REACH * STRETCH + ROWS
WINDOW = (REACH + 1) * STRETCH
GROUP = 8
SKIPS = (512, 256, 0)
PADDED = HEAD_DIM + 16
EXPONENT_SCALE = HEAD_DIM ** (-0.5) * 1.4426950408889634
SMALL, LARGE = 2.0**-60, 2.0**110
VMEM_LIMIT = 24 << 20
VMEM_SPEC = pl.BlockSpec(memory_space=pltpu.VMEM)
ANY_SPEC = pl.BlockSpec(memory_space=pl.ANY)
SMEM_SPEC = pl.BlockSpec(memory_space=pltpu.SMEM)
PARAMS = pltpu.CompilerParams(vmem_limit_bytes=VMEM_LIMIT)


def kv_pack_kernel(key_ref, value_ref, out_ref, stage, sems):
    width = key_ref.shape[1] // HEADS
    loads = [
        pltpu.make_async_copy(source, stage.at[kind], sems.at[kind, HEADS])
        for kind, source in enumerate((key_ref, value_ref))
    ]
    for load in loads:
        load.start()
    stores = []
    for kind, load in enumerate(loads):
        load.wait()
        for dest in range(HEADS):
            store = pltpu.make_async_copy(
                stage.at[kind, :, pl.ds(dest * width, width)],
                out_ref.at[dest, :, pl.ds(kind * width, width)],
                sems.at[kind, dest],
            )
            store.start()
            stores.append(store)
    for store in stores:
        store.wait()


def kv_pack(key_rows, value_rows):
    rows, width = key_rows.shape
    return pl.pallas_call(
        kv_pack_kernel,
        in_specs=[ANY_SPEC, ANY_SPEC],
        out_specs=ANY_SPEC,
        out_shape=jax.ShapeDtypeStruct((HEADS, rows, 2 * width // HEADS), key_rows.dtype),
        scratch_shapes=[
            pltpu.VMEM((2, rows, width), key_rows.dtype),
            pltpu.SemaphoreType.DMA((2, HEADS + 1)),
        ],
        compiler_params=pltpu.CompilerParams(vmem_limit_bytes=60 << 20),
        name="kv_pack",
    )(key_rows, value_rows)


def query_pack_kernel(count, place_ref, lengths_ref, query_ref, *refs):
    out_ref, starts_ref, reach_ref, sems = refs
    width = query_ref.shape[1] // HEADS
    copies = [
        pltpu.make_async_copy(
            query_ref.at[:, pl.ds(dest * width, width)], out_ref.at[dest], sems.at[dest]
        )
        for dest in range(HEADS)
    ]
    for copy in copies:
        copy.start()
    docs = lengths_ref.shape[1]
    earlier = lax.broadcasted_iota(jnp.int32, (docs, docs), 1) < lax.broadcasted_iota(
        jnp.int32, (docs, docs), 0
    )
    starts = 2 * jnp.sum(jnp.where(earlier, lengths_ref[...], 0), axis=1, keepdims=True)
    starts_ref[...] = starts
    ctx = place_ref[0]
    for block in range(HEADS):
        stretch = ctx if block < 2 else 2 * count - 1 - ctx
        first = stretch * STRETCH + block % 2 * ROWS
        reach_ref[block] = first - jnp.max(jnp.where(starts <= first, starts, 0))
    for copy in copies:
        copy.wait()


def query_pack(count, place, lengths, queries):
    rows, width = queries.shape
    packed = jax.ShapeDtypeStruct((HEADS, rows, width // HEADS), queries.dtype)
    return pl.pallas_call(
        functools.partial(query_pack_kernel, count),
        in_specs=[SMEM_SPEC, VMEM_SPEC, ANY_SPEC],
        out_specs=[VMEM_SPEC] * 2 + [SMEM_SPEC],
        out_shape=[
            packed,
            jax.ShapeDtypeStruct((lengths.shape[1], 1), jnp.int32),
            jax.ShapeDtypeStruct((HEADS,), jnp.int32),
        ],
        scratch_shapes=[pltpu.SemaphoreType.DMA((HEADS,))],
        compiler_params=PARAMS,
        name="query_pack",
    )(place, lengths, queries)


def load_windows(ctx, count, own, up, down, far, inner, mate_up, mate_down, keys, values, sems):
    odd = lax.rem(ctx, 2) == 1
    even = jnp.logical_not(odd)
    last = ctx == count - 1
    before_last = ctx == count - 2
    plain = ctx < count - 2
    width = keys.shape[2]

    def piece(kind, source, row, lane, slot):
        return pltpu.make_async_copy(
            source.at[pl.ds(row, STRETCH), pl.ds((1 - kind) * width, width)],
            (values, keys)[kind].at[lane, pl.ds(slot * STRETCH, STRETCH), :],
            sems.at[kind, lane, slot],
        )

    def start(condition, source, row, lane, slot):
        @pl.when(condition)
        def _():
            for kind in range(2):
                piece(kind, source, row, lane, slot).start()

    for lane in range(LANES):
        for kind in range(2):
            piece(kind, own, lane * STRETCH, lane, 3).start()
    for kind in range(2):
        piece(kind, up, 0, 0, 1).start()
    start(odd, mate_up, 0, 0, 0)
    start(even, far, 0, 0, 0)
    start(odd, inner, 0, 0, 2)
    start(even, mate_up, 0, 0, 2)
    start(jnp.logical_and(even, plain), mate_down, 0, 1, 0)
    start(jnp.logical_and(odd, plain), far, 0, 1, 0)
    start(before_last, own, 0, 1, 0)
    start(last, up, 0, 1, 0)
    start(plain, down, 0, 1, 1)
    start(before_last, mate_down, 0, 1, 1)
    start(last, inner, 0, 1, 1)
    start(even, inner, 0, 1, 2)
    start(jnp.logical_and(odd, plain), mate_down, 0, 1, 2)
    start(last, own, 0, 1, 2)

    def wait(kind, lane):
        for slot in range(REACH + 1):
            piece(kind, own, 0, lane, slot).wait()

    return wait


def attention_kernel(
    count, place_ref, starts_ref, reach_ref, own, up, down, far, inner, mate_up, mate_down,
    query_all,
    out_ref, keys, values, values_t, query, result, bias, flags, sems, load_sems, store_sems,
):
    ctx = place_ref[0]
    width = query.shape[2]
    kv_local = keys.shape[2] // HEAD_DIM
    part_width = width // kv_local
    wait = load_windows(
        ctx, count, own, up, down, far, inner, mate_up, mate_down, keys, values, sems
    )

    loads = [
        pltpu.make_async_copy(query_all.at[block], query.at[block], load_sems.at[block])
        for block in range(HEADS)
    ]
    for copy in loads:
        copy.start()
    flags[...] = jnp.zeros_like(flags)

    def store(block, kv_head):
        rows = pl.ds(pl.multiple_of(block * ROWS, ROWS), ROWS)
        cols = pl.ds(kv_head * part_width, part_width)
        return pltpu.make_async_copy(
            result.at[block, :, cols], out_ref.at[rows, cols], store_sems.at[block, kv_head]
        )

    def set_bias(block):
        lane, half = block // 2, lax.rem(block, 2)
        stretch = jnp.where(lane == 0, ctx, 2 * count - 1 - ctx)
        first = stretch * STRETCH + half * ROWS
        starts = starts_ref[...]
        row_pos = first + lax.broadcasted_iota(jnp.int32, (1, ROWS), 1)
        row_start = jnp.max(jnp.where(starts <= row_pos, starts, 0), axis=0, keepdims=True)
        key_pos = first - REACH * STRETCH + lax.broadcasted_iota(jnp.int32, (KEYS, ROWS), 0)
        allowed = (key_pos >= row_start) & (key_pos <= row_pos)
        bias[...] = jnp.where(allowed, 0.0, -jnp.inf).astype(jnp.float32)

    def part(block, kv_head, base, heads, raise_by, skip=0):
        lane, half = block // 2, lax.rem(block, 2)
        window = pl.ds(pl.multiple_of(half * ROWS + skip, ROWS), KEYS - skip)
        cols = [pl.ds(base + at * HEAD_DIM, HEAD_DIM) for at in range(heads)]
        stacked = jnp.concatenate([query[block, :, col] for col in cols], axis=0)
        key = keys[lane, window, kv_head * HEAD_DIM : (kv_head + 1) * HEAD_DIM]
        scores = lax.dot_general(
            key, stacked, (((1,), (1,)), ((), ())), preferred_element_type=jnp.float32
        )
        masks = jnp.concatenate([bias[skip:]] * heads, axis=1)
        weights = jnp.exp2(raise_by(scores, masks)).astype(jnp.bfloat16)
        mixed = jnp.dot(
            values_t[lane, kv_head, :, window], weights, preferred_element_type=jnp.float32
        )
        total = mixed[HEAD_DIM : HEAD_DIM + 1]
        part_result = (mixed[:HEAD_DIM] / total).astype(out_ref.dtype)
        for at, col in enumerate(cols):
            result[block, :, col] = part_result[:, at * HEAD_DIM : (at + 1) * HEAD_DIM].T
        return total

    for lane in range(LANES):
        wait(0, lane)
        for kv_head in range(kv_local):
            values_t[lane, kv_head, :HEAD_DIM, :] = values[
                lane, :, kv_head * HEAD_DIM : (kv_head + 1) * HEAD_DIM
            ].T
            values_t[lane, kv_head, HEAD_DIM:, :] = jnp.ones(
                (PADDED - HEAD_DIM, WINDOW), values_t.dtype
            )
    for lane in range(LANES):
        wait(1, lane)
    for copy in loads:
        copy.wait()

    @pl.loop(0, HEADS)
    def _(block):
        set_bias(block)
        reach = reach_ref[block]

        def run(skip, condition):
            @pl.when(condition)
            def _():
                for kv_head in range(kv_local):
                    total = part(
                        block, kv_head, kv_head * part_width, GROUP,
                        lambda scores, masks: scores * EXPONENT_SCALE + masks, skip,
                    )
                    inside = (total >= SMALL) & (total <= LARGE)
                    flags[...] = jnp.maximum(flags[...], jnp.where(inside, 0.0, 1.0))
                    store(block, kv_head).start()

        room = REACH * STRETCH
        low = 0
        for skip in SKIPS:
            run(skip, (reach > low) & (reach <= room - skip) if low else reach <= room - skip)
            low = room - skip

    for block in range(HEADS):
        for kv_head in range(kv_local):
            store(block, kv_head).wait()

    @pl.when(jnp.max(flags[...]) > 0)
    def _():
        def shifted(scores, masks):
            scores = scores + masks
            return (scores - jnp.max(scores, axis=0, keepdims=True)) * EXPONENT_SCALE

        @pl.loop(0, HEADS)
        def _(block):
            set_bias(block)
            for kv_head in range(kv_local):

                @pl.loop(0, GROUP)
                def _(head):
                    base = pl.multiple_of(kv_head * part_width + head * HEAD_DIM, HEAD_DIM)
                    part(block, kv_head, base, 1, shifted)

                copy = store(block, kv_head)
                copy.start()
                copy.wait()


def attention(
    count, place, starts, reach, own, up, down, far, inner, mate_up, mate_down,
    query,
):
    _, rows, width = query.shape
    kv_width = own.shape[1] // 2
    kv_local = kv_width // HEAD_DIM
    dtype = query.dtype
    return pl.pallas_call(
        functools.partial(attention_kernel, count),
        in_specs=[SMEM_SPEC, VMEM_SPEC, SMEM_SPEC] + [VMEM_SPEC] * 7 + [ANY_SPEC],
        out_specs=ANY_SPEC,
        out_shape=jax.ShapeDtypeStruct((HEADS * rows, width), dtype),
        scratch_shapes=[
            pltpu.VMEM((LANES, WINDOW, kv_width), dtype),
            pltpu.VMEM((LANES, WINDOW, kv_width), dtype),
            pltpu.VMEM((LANES, kv_local, PADDED, WINDOW), dtype),
            pltpu.VMEM((HEADS, rows, width), dtype),
            pltpu.VMEM((HEADS, rows, width), dtype),
            pltpu.VMEM((KEYS, ROWS), jnp.float32),
            pltpu.VMEM((1, GROUP * ROWS), jnp.float32),
            pltpu.SemaphoreType.DMA((2, LANES, REACH + 1)),
            pltpu.SemaphoreType.DMA((HEADS,)),
            pltpu.SemaphoreType.DMA((HEADS, kv_local)),
        ],
        compiler_params=PARAMS,
        name="attention",
    )(
        place, starts, reach, own, up, down, far, inner, mate_up, mate_down,
        query,
    )


def body(queries, key_rows, value_rows, doc_lengths):
    count = lax.axis_size("ctx")
    ctx = lax.axis_index("ctx")
    odd = lax.rem(ctx, 2) == 1
    place = jnp.stack([ctx, lax.axis_index("head")])

    packed = kv_pack(key_rows, value_rows)
    by_head, starts, reach = query_pack(count, place, doc_lengths.reshape(1, -1), queries)
    kv = lax.all_to_all(packed, "head", split_axis=0, concat_axis=0, tiled=True)
    kv = kv.reshape(LANES * STRETCH, -1)

    query = lax.all_to_all(by_head, "head", split_axis=0, concat_axis=0, tiled=True)
    lane0, lane1 = kv[:STRETCH], kv[STRETCH:]
    last = ctx == count - 1
    swap = [(i, i ^ 1) for i in range(count)]
    up = lax.ppermute(lane0, "ctx", [(i, i + 2) for i in range(count - 2)])
    down = lax.ppermute(lane1, "ctx", [(i + 2, i) for i in range(count - 2)])
    route = [(i, i + 3) for i in range(1, count - 3, 2)]
    route += [(i + 3, i) for i in range(1, count - 3, 2)]
    route += [(count - 1, count - 3)]
    far = lax.ppermute(jnp.where(odd, lane0, lane1), "ctx", route)
    inner = lax.ppermute(jnp.where(odd, lane1, lane0), "ctx", swap)
    inner = lax.ppermute(jnp.where(odd, lane1, lane0), "ctx", swap)
    inner, down, far, up = lax.optimization_barrier((inner, down, far, up))
    mate_up = lax.ppermute(up, "ctx", swap)
    mate_down = lax.ppermute(jnp.where(last, lane0, down), "ctx", swap)
    return attention(
        count, place, starts, reach, kv, up, down, far, inner, mate_up, mate_down, query
    )


def solution(mesh):
    placed = (P(("ctx", "head"), None), P(("ctx", "head"), None), P(("ctx", "head"), None), P())
    return jax.shard_map(
        body, mesh=mesh, in_specs=placed, out_specs=P("ctx", "head"), check_vma=False
    )
```

```python
import functools
import jax
import jax.numpy as jnp
from jax import lax
from jax.experimental import pallas as pl
from jax.experimental.pallas import tpu as pltpu
from jax.sharding import PartitionSpec as P

HEAD_DIM = 128
REACH = 3
STRETCH = 256
LANES = 2
HEADS = 4
ROWS = 128
KEYS = REACH * STRETCH + ROWS
WINDOW = (REACH + 1) * STRETCH
GROUP = 8
SKIPS = (512, 256, 0)
PADDED = HEAD_DIM + 16
EXPONENT_SCALE = HEAD_DIM ** (-0.5) * 1.4426950408889634
SMALL, LARGE = 2.0**-60, 2.0**110
VMEM_LIMIT = 24 << 20
VMEM_SPEC = pl.BlockSpec(memory_space=pltpu.VMEM)
ANY_SPEC = pl.BlockSpec(memory_space=pl.ANY)
SMEM_SPEC = pl.BlockSpec(memory_space=pltpu.SMEM)
PARAMS = pltpu.CompilerParams(vmem_limit_bytes=VMEM_LIMIT)


def kv_pack_kernel(key_ref, value_ref, out_ref, sems):
    width = key_ref.shape[1] // HEADS
    copies = [
        pltpu.make_async_copy(
            source.at[:, pl.ds(dest * width, width)],
            out_ref.at[dest, :, pl.ds(kind * width, width)],
            sems.at[kind, dest],
        )
        for kind, source in enumerate((key_ref, value_ref))
        for dest in range(HEADS)
    ]
    for copy in copies:
        copy.start()
    for copy in copies:
        copy.wait()


def kv_pack(key_rows, value_rows):
    rows, width = key_rows.shape
    hbm = pl.BlockSpec(memory_space=pltpu.HBM)
    return pl.pallas_call(
        kv_pack_kernel,
        in_specs=[hbm, hbm],
        out_specs=VMEM_SPEC,
        out_shape=jax.ShapeDtypeStruct((HEADS, rows, 2 * width // HEADS), key_rows.dtype),
        scratch_shapes=[pltpu.SemaphoreType.DMA((2, HEADS))],
        compiler_params=PARAMS,
        name="kv_pack",
    )(
        pltpu.with_memory_space_constraint(key_rows, pltpu.HBM),
        pltpu.with_memory_space_constraint(value_rows, pltpu.HBM),
    )


def query_pack_kernel(count, place_ref, lengths_ref, query_ref, *refs):
    out_refs, starts_ref, reach_ref, sems = refs[:-3], refs[-3], refs[-2], refs[-1]
    width = query_ref.shape[1] // HEADS
    copies = []
    for at, (shift, out_ref) in enumerate(zip((1, 3, 2), out_refs)):
        col = pl.multiple_of(lax.rem(place_ref[1] + shift, HEADS) * width, width)
        copies.append(
            pltpu.make_async_copy(query_ref.at[:, pl.ds(col, width)], out_ref, sems.at[at])
        )
    for copy in copies:
        copy.start()
    docs = lengths_ref.shape[1]
    earlier = lax.broadcasted_iota(jnp.int32, (docs, docs), 1) < lax.broadcasted_iota(
        jnp.int32, (docs, docs), 0
    )
    starts = 2 * jnp.sum(jnp.where(earlier, lengths_ref[...], 0), axis=1, keepdims=True)
    starts_ref[...] = starts
    ctx = place_ref[0]
    for block in range(HEADS):
        stretch = ctx if block < 2 else 2 * count - 1 - ctx
        first = stretch * STRETCH + block % 2 * ROWS
        reach_ref[block] = first - jnp.max(jnp.where(starts <= first, starts, 0))
    for copy in copies:
        copy.wait()


def query_pack(count, place, lengths, queries):
    rows, width = queries.shape
    block = jax.ShapeDtypeStruct((rows, width // HEADS), queries.dtype)
    return pl.pallas_call(
        functools.partial(query_pack_kernel, count),
        in_specs=[SMEM_SPEC, VMEM_SPEC, ANY_SPEC],
        out_specs=[VMEM_SPEC] * 4 + [SMEM_SPEC],
        out_shape=[block] * 3 + [
            jax.ShapeDtypeStruct((lengths.shape[1], 1), jnp.int32),
            jax.ShapeDtypeStruct((HEADS,), jnp.int32),
        ],
        scratch_shapes=[pltpu.SemaphoreType.DMA((3,))],
        compiler_params=PARAMS,
        name="query_pack",
    )(place, lengths, queries)


def load_windows(ctx, count, own, up, down, far, inner, mate_up, mate_down, keys, values, sems):
    odd = lax.rem(ctx, 2) == 1
    even = jnp.logical_not(odd)
    last = ctx == count - 1
    before_last = ctx == count - 2
    plain = ctx < count - 2
    width = keys.shape[2]

    def piece(kind, source, row, lane, slot):
        return pltpu.make_async_copy(
            source.at[pl.ds(row, STRETCH), pl.ds((1 - kind) * width, width)],
            (values, keys)[kind].at[lane, pl.ds(slot * STRETCH, STRETCH), :],
            sems.at[kind, lane, slot],
        )

    def start(condition, source, row, lane, slot):
        @pl.when(condition)
        def _():
            for kind in range(2):
                piece(kind, source, row, lane, slot).start()

    for lane in range(LANES):
        for kind in range(2):
            piece(kind, own, lane * STRETCH, lane, 3).start()
    for kind in range(2):
        piece(kind, up, 0, 0, 1).start()
    start(odd, mate_up, 0, 0, 0)
    start(even, far, 0, 0, 0)
    start(odd, inner, 0, 0, 2)
    start(even, mate_up, 0, 0, 2)
    start(jnp.logical_and(even, plain), mate_down, 0, 1, 0)
    start(jnp.logical_and(odd, plain), far, 0, 1, 0)
    start(before_last, own, 0, 1, 0)
    start(last, up, 0, 1, 0)
    start(plain, down, 0, 1, 1)
    start(before_last, mate_down, 0, 1, 1)
    start(last, inner, 0, 1, 1)
    start(even, inner, 0, 1, 2)
    start(jnp.logical_and(odd, plain), mate_down, 0, 1, 2)
    start(last, own, 0, 1, 2)

    def wait(kind, lane):
        for slot in range(REACH + 1):
            piece(kind, own, 0, lane, slot).wait()

    return wait


def attention_kernel(
    count, place_ref, starts_ref, reach_ref, own, up, down, far, inner, mate_up, mate_down,
    queries, left, right, across,
    out_ref, keys, values, values_t, query, result, bias, flags, sems, load_sems, store_sems,
):
    ctx, head = place_ref[0], place_ref[1]
    width = query.shape[2]
    kv_local = keys.shape[2] // HEAD_DIM
    part_width = width // kv_local
    wait = load_windows(
        ctx, count, own, up, down, far, inner, mate_up, mate_down, keys, values, sems
    )

    def load(shift, source):
        block = lax.rem(head + HEADS - shift, HEADS)
        return pltpu.make_async_copy(source, query.at[block], load_sems.at[shift])

    own_cols = pl.ds(pl.multiple_of(head * width, width), width)
    loads = [
        load(shift, source)
        for shift, source in enumerate((queries.at[:, own_cols], left, across, right))
    ]
    for copy in loads:
        copy.start()
    flags[...] = jnp.zeros_like(flags)

    def store(block, kv_head):
        rows = pl.ds(pl.multiple_of(block * ROWS, ROWS), ROWS)
        cols = pl.ds(kv_head * part_width, part_width)
        return pltpu.make_async_copy(
            result.at[block, :, cols], out_ref.at[rows, cols], store_sems.at[block, kv_head]
        )

    def set_bias(block):
        lane, half = block // 2, lax.rem(block, 2)
        stretch = jnp.where(lane == 0, ctx, 2 * count - 1 - ctx)
        first = stretch * STRETCH + half * ROWS
        starts = starts_ref[...]
        row_pos = first + lax.broadcasted_iota(jnp.int32, (1, ROWS), 1)
        row_start = jnp.max(jnp.where(starts <= row_pos, starts, 0), axis=0, keepdims=True)
        key_pos = first - REACH * STRETCH + lax.broadcasted_iota(jnp.int32, (KEYS, ROWS), 0)
        allowed = (key_pos >= row_start) & (key_pos <= row_pos)
        bias[...] = jnp.where(allowed, 0.0, -jnp.inf).astype(jnp.float32)

    def part(block, kv_head, base, heads, raise_by, skip=0):
        lane, half = block // 2, lax.rem(block, 2)
        window = pl.ds(pl.multiple_of(half * ROWS + skip, ROWS), KEYS - skip)
        cols = [pl.ds(base + at * HEAD_DIM, HEAD_DIM) for at in range(heads)]
        stacked = jnp.concatenate([query[block, :, col] for col in cols], axis=0)
        key = keys[lane, window, kv_head * HEAD_DIM : (kv_head + 1) * HEAD_DIM]
        scores = lax.dot_general(
            key, stacked, (((1,), (1,)), ((), ())), preferred_element_type=jnp.float32
        )
        masks = jnp.concatenate([bias[skip:]] * heads, axis=1)
        weights = jnp.exp2(raise_by(scores, masks)).astype(jnp.bfloat16)
        mixed = jnp.dot(
            values_t[lane, kv_head, :, window], weights, preferred_element_type=jnp.float32
        )
        total = mixed[HEAD_DIM : HEAD_DIM + 1]
        part_result = (mixed[:HEAD_DIM] / total).astype(out_ref.dtype)
        for at, col in enumerate(cols):
            result[block, :, col] = part_result[:, at * HEAD_DIM : (at + 1) * HEAD_DIM].T
        return total

    for lane in range(LANES):
        wait(0, lane)
        for kv_head in range(kv_local):
            values_t[lane, kv_head, :HEAD_DIM, :] = values[
                lane, :, kv_head * HEAD_DIM : (kv_head + 1) * HEAD_DIM
            ].T
            values_t[lane, kv_head, HEAD_DIM:, :] = jnp.ones(
                (PADDED - HEAD_DIM, WINDOW), values_t.dtype
            )
    for lane in range(LANES):
        wait(1, lane)
    for copy in loads:
        copy.wait()

    @pl.loop(0, HEADS)
    def _(block):
        set_bias(block)
        reach = reach_ref[block]

        def run(skip, condition):
            @pl.when(condition)
            def _():
                for kv_head in range(kv_local):
                    total = part(
                        block, kv_head, kv_head * part_width, GROUP,
                        lambda scores, masks: scores * EXPONENT_SCALE + masks, skip,
                    )
                    inside = (total >= SMALL) & (total <= LARGE)
                    flags[...] = jnp.maximum(flags[...], jnp.where(inside, 0.0, 1.0))
                    store(block, kv_head).start()

        room = REACH * STRETCH
        low = 0
        for skip in SKIPS:
            run(skip, (reach > low) & (reach <= room - skip) if low else reach <= room - skip)
            low = room - skip

    for block in range(HEADS):
        for kv_head in range(kv_local):
            store(block, kv_head).wait()

    @pl.when(jnp.max(flags[...]) > 0)
    def _():
        def shifted(scores, masks):
            scores = scores + masks
            return (scores - jnp.max(scores, axis=0, keepdims=True)) * EXPONENT_SCALE

        @pl.loop(0, HEADS)
        def _(block):
            set_bias(block)
            for kv_head in range(kv_local):

                @pl.loop(0, GROUP)
                def _(head):
                    base = pl.multiple_of(kv_head * part_width + head * HEAD_DIM, HEAD_DIM)
                    part(block, kv_head, base, 1, shifted)

                copy = store(block, kv_head)
                copy.start()
                copy.wait()


def attention(
    count, place, starts, reach, own, up, down, far, inner, mate_up, mate_down,
    queries, left, right, across,
):
    rows, width = left.shape
    kv_width = own.shape[1] // 2
    kv_local = kv_width // HEAD_DIM
    dtype = queries.dtype
    return pl.pallas_call(
        functools.partial(attention_kernel, count),
        in_specs=[SMEM_SPEC, VMEM_SPEC, SMEM_SPEC] + [VMEM_SPEC] * 7 + [ANY_SPEC] * 4,
        out_specs=ANY_SPEC,
        out_shape=jax.ShapeDtypeStruct((HEADS * rows, width), dtype),
        scratch_shapes=[
            pltpu.VMEM((LANES, WINDOW, kv_width), dtype),
            pltpu.VMEM((LANES, WINDOW, kv_width), dtype),
            pltpu.VMEM((LANES, kv_local, PADDED, WINDOW), dtype),
            pltpu.VMEM((HEADS, rows, width), dtype),
            pltpu.VMEM((HEADS, rows, width), dtype),
            pltpu.VMEM((KEYS, ROWS), jnp.float32),
            pltpu.VMEM((1, GROUP * ROWS), jnp.float32),
            pltpu.SemaphoreType.DMA((2, LANES, REACH + 1)),
            pltpu.SemaphoreType.DMA((HEADS,)),
            pltpu.SemaphoreType.DMA((HEADS, kv_local)),
        ],
        compiler_params=PARAMS,
        name="attention",
    )(
        place, starts, reach, own, up, down, far, inner, mate_up, mate_down,
        queries, left, right, across,
    )


def body(queries, key_rows, value_rows, doc_lengths):
    count = lax.axis_size("ctx")
    ctx = lax.axis_index("ctx")
    odd = lax.rem(ctx, 2) == 1
    place = jnp.stack([ctx, lax.axis_index("head")])

    packed = kv_pack(key_rows, value_rows)
    to_next, to_previous, to_opposite, starts, reach = query_pack(count, place, doc_lengths.reshape(1, -1), queries)
    kv = lax.all_to_all(packed, "head", split_axis=0, concat_axis=0, tiled=True)
    kv = kv.reshape(LANES * STRETCH, -1)

    def rotate(block, shift):
        return lax.ppermute(block, "head", [(i, (i + shift) % HEADS) for i in range(HEADS)])

    kv, starts = lax.optimization_barrier((kv, starts))
    left = rotate(to_next, 1)
    right = rotate(to_previous, 3)
    across = rotate(to_opposite, 2)

    lane0, lane1 = kv[:STRETCH], kv[STRETCH:]
    last = ctx == count - 1
    swap = [(i, i ^ 1) for i in range(count)]
    up = lax.ppermute(lane0, "ctx", [(i, i + 2) for i in range(count - 2)])
    down = lax.ppermute(lane1, "ctx", [(i + 2, i) for i in range(count - 2)])
    route = [(i, i + 3) for i in range(1, count - 3, 2)]
    route += [(i + 3, i) for i in range(1, count - 3, 2)]
    route += [(count - 1, count - 3)]
    far = lax.ppermute(jnp.where(odd, lane0, lane1), "ctx", route)
    inner = lax.ppermute(jnp.where(odd, lane1, lane0), "ctx", swap)
    down, far, up, left, right = lax.optimization_barrier((down, far, up, left, right))
    mate_up = lax.ppermute(up, "ctx", swap)
    mate_down = lax.ppermute(jnp.where(last, lane0, down), "ctx", swap)
    return attention(
        count, place, starts, reach, kv, up, down, far, inner, mate_up, mate_down, queries, left, right, across
    )


def solution(mesh):
    placed = (P(("ctx", "head"), None), P(("ctx", "head"), None), P(("ctx", "head"), None), P())
    return jax.shard_map(
        body, mesh=mesh, in_specs=placed, out_specs=P("ctx", "head"), check_vma=False
    )
```

```python
import functools
import jax
import jax.numpy as jnp
from jax import lax
from jax.experimental import pallas as pl
from jax.experimental.pallas import tpu as pltpu
from jax.sharding import PartitionSpec as P

HEAD_DIM = 128
REACH = 3
STRETCH = 256
LANES = 2
HEADS = 4
ROWS = 128
KEYS = REACH * STRETCH + ROWS
WINDOW = (REACH + 1) * STRETCH
GROUP = 8
SKIPS = (512, 384, 256, 128, 0)
PADDED = HEAD_DIM + 16
EXPONENT_SCALE = HEAD_DIM ** (-0.5) * 1.4426950408889634
SMALL, LARGE = 2.0**-60, 2.0**110
VMEM_LIMIT = 24 << 20
VMEM_SPEC = pl.BlockSpec(memory_space=pltpu.VMEM)
ANY_SPEC = pl.BlockSpec(memory_space=pl.ANY)
SMEM_SPEC = pl.BlockSpec(memory_space=pltpu.SMEM)
PARAMS = pltpu.CompilerParams(vmem_limit_bytes=VMEM_LIMIT)


def kv_pack_kernel(key_ref, value_ref, out_ref, stage, sems):
    width = key_ref.shape[1] // HEADS
    loads = [
        pltpu.make_async_copy(source, stage.at[kind], sems.at[kind, HEADS])
        for kind, source in enumerate((key_ref, value_ref))
    ]
    for load in loads:
        load.start()
    stores = []
    for kind, load in enumerate(loads):
        load.wait()
        for dest in range(HEADS):
            store = pltpu.make_async_copy(
                stage.at[kind, :, pl.ds(dest * width, width)],
                out_ref.at[dest, :, pl.ds(kind * width, width)],
                sems.at[kind, dest],
            )
            store.start()
            stores.append(store)
    for store in stores:
        store.wait()


def kv_pack(key_rows, value_rows):
    rows, width = key_rows.shape
    return pl.pallas_call(
        kv_pack_kernel,
        in_specs=[ANY_SPEC, ANY_SPEC],
        out_specs=ANY_SPEC,
        out_shape=jax.ShapeDtypeStruct((HEADS, rows, 2 * width // HEADS), key_rows.dtype),
        scratch_shapes=[
            pltpu.VMEM((2, rows, width), key_rows.dtype),
            pltpu.SemaphoreType.DMA((2, HEADS + 1)),
        ],
        compiler_params=pltpu.CompilerParams(vmem_limit_bytes=60 << 20),
        name="kv_pack",
    )(key_rows, value_rows)


def query_pack_kernel(count, place_ref, lengths_ref, query_ref, *refs):
    out_refs, starts_ref, reach_ref, sems = refs[:-3], refs[-3], refs[-2], refs[-1]
    width = query_ref.shape[1] // HEADS
    copies = []
    for at, (shift, out_ref) in enumerate(zip((1, 3, 2), out_refs)):
        col = pl.multiple_of(lax.rem(place_ref[1] + shift, HEADS) * width, width)
        copies.append(
            pltpu.make_async_copy(query_ref.at[:, pl.ds(col, width)], out_ref, sems.at[at])
        )
    for copy in copies:
        copy.start()
    docs = lengths_ref.shape[1]
    earlier = lax.broadcasted_iota(jnp.int32, (docs, docs), 1) < lax.broadcasted_iota(
        jnp.int32, (docs, docs), 0
    )
    starts = 2 * jnp.sum(jnp.where(earlier, lengths_ref[...], 0), axis=1, keepdims=True)
    starts_ref[...] = starts
    ctx = place_ref[0]
    for block in range(HEADS):
        stretch = ctx if block < 2 else 2 * count - 1 - ctx
        first = stretch * STRETCH + block % 2 * ROWS
        reach_ref[block] = first - jnp.max(jnp.where(starts <= first, starts, 0))
    for copy in copies:
        copy.wait()


def query_pack(count, place, lengths, queries):
    rows, width = queries.shape
    block = jax.ShapeDtypeStruct((rows, width // HEADS), queries.dtype)
    return pl.pallas_call(
        functools.partial(query_pack_kernel, count),
        in_specs=[SMEM_SPEC, VMEM_SPEC, ANY_SPEC],
        out_specs=[VMEM_SPEC] * 4 + [SMEM_SPEC],
        out_shape=[block] * 3 + [
            jax.ShapeDtypeStruct((lengths.shape[1], 1), jnp.int32),
            jax.ShapeDtypeStruct((HEADS,), jnp.int32),
        ],
        scratch_shapes=[pltpu.SemaphoreType.DMA((3,))],
        compiler_params=PARAMS,
        name="query_pack",
    )(place, lengths, queries)


def load_windows(ctx, count, own, up, down, far, inner, mate_up, mate_down, keys, values, sems):
    odd = lax.rem(ctx, 2) == 1
    even = jnp.logical_not(odd)
    last = ctx == count - 1
    before_last = ctx == count - 2
    plain = ctx < count - 2
    width = keys.shape[2]

    def piece(kind, source, row, lane, slot):
        return pltpu.make_async_copy(
            source.at[pl.ds(row, STRETCH), pl.ds((1 - kind) * width, width)],
            (values, keys)[kind].at[lane, pl.ds(slot * STRETCH, STRETCH), :],
            sems.at[kind, lane, slot],
        )

    def start(condition, source, row, lane, slot):
        @pl.when(condition)
        def _():
            for kind in range(2):
                piece(kind, source, row, lane, slot).start()

    for lane in range(LANES):
        for kind in range(2):
            piece(kind, own, lane * STRETCH, lane, 3).start()
    for kind in range(2):
        piece(kind, up, 0, 0, 1).start()
    start(odd, mate_up, 0, 0, 0)
    start(even, far, 0, 0, 0)
    start(odd, inner, 0, 0, 2)
    start(even, mate_up, 0, 0, 2)
    start(jnp.logical_and(even, plain), mate_down, 0, 1, 0)
    start(jnp.logical_and(odd, plain), far, 0, 1, 0)
    start(before_last, own, 0, 1, 0)
    start(last, up, 0, 1, 0)
    start(plain, down, 0, 1, 1)
    start(before_last, mate_down, 0, 1, 1)
    start(last, inner, 0, 1, 1)
    start(even, inner, 0, 1, 2)
    start(jnp.logical_and(odd, plain), mate_down, 0, 1, 2)
    start(last, own, 0, 1, 2)

    def wait(kind, lane):
        for slot in range(REACH + 1):
            piece(kind, own, 0, lane, slot).wait()

    return wait


def attention_kernel(
    count, place_ref, starts_ref, reach_ref, own, up, down, far, inner, mate_up, mate_down,
    queries, left, right, across,
    out_ref, keys, values, values_t, query, result, bias, flags, sems, load_sems, store_sems,
):
    ctx, head = place_ref[0], place_ref[1]
    width = query.shape[2]
    kv_local = keys.shape[2] // HEAD_DIM
    part_width = width // kv_local
    wait = load_windows(
        ctx, count, own, up, down, far, inner, mate_up, mate_down, keys, values, sems
    )

    def load(shift, source):
        block = lax.rem(head + HEADS - shift, HEADS)
        return pltpu.make_async_copy(source, query.at[block], load_sems.at[shift])

    own_cols = pl.ds(pl.multiple_of(head * width, width), width)
    loads = [
        load(shift, source)
        for shift, source in enumerate((queries.at[:, own_cols], left, across, right))
    ]
    for copy in loads:
        copy.start()
    flags[...] = jnp.zeros_like(flags)

    def store(block, kv_head):
        rows = pl.ds(pl.multiple_of(block * ROWS, ROWS), ROWS)
        cols = pl.ds(kv_head * part_width, part_width)
        return pltpu.make_async_copy(
            result.at[block, :, cols], out_ref.at[rows, cols], store_sems.at[block, kv_head]
        )

    def set_bias(block):
        lane, half = block // 2, lax.rem(block, 2)
        stretch = jnp.where(lane == 0, ctx, 2 * count - 1 - ctx)
        first = stretch * STRETCH + half * ROWS
        starts = starts_ref[...]
        row_pos = first + lax.broadcasted_iota(jnp.int32, (1, ROWS), 1)
        row_start = jnp.max(jnp.where(starts <= row_pos, starts, 0), axis=0, keepdims=True)
        key_pos = first - REACH * STRETCH + lax.broadcasted_iota(jnp.int32, (KEYS, ROWS), 0)
        allowed = (key_pos >= row_start) & (key_pos <= row_pos)
        bias[...] = jnp.where(allowed, 0.0, -jnp.inf).astype(jnp.float32)

    def part(block, kv_head, base, heads, raise_by, skip=0):
        lane, half = block // 2, lax.rem(block, 2)
        window = pl.ds(pl.multiple_of(half * ROWS + skip, ROWS), KEYS - skip)
        cols = [pl.ds(base + at * HEAD_DIM, HEAD_DIM) for at in range(heads)]
        stacked = jnp.concatenate([query[block, :, col] for col in cols], axis=0)
        key = keys[lane, window, kv_head * HEAD_DIM : (kv_head + 1) * HEAD_DIM]
        scores = lax.dot_general(
            key, stacked, (((1,), (1,)), ((), ())), preferred_element_type=jnp.float32
        )
        masks = jnp.concatenate([bias[skip:]] * heads, axis=1)
        weights = jnp.exp2(raise_by(scores, masks)).astype(jnp.bfloat16)
        mixed = jnp.dot(
            values_t[lane, kv_head, :, window], weights, preferred_element_type=jnp.float32
        )
        total = mixed[HEAD_DIM : HEAD_DIM + 1]
        part_result = (mixed[:HEAD_DIM] / total).astype(out_ref.dtype)
        for at, col in enumerate(cols):
            result[block, :, col] = part_result[:, at * HEAD_DIM : (at + 1) * HEAD_DIM].T
        return total

    for lane in range(LANES):
        wait(0, lane)
        for kv_head in range(kv_local):
            values_t[lane, kv_head, :HEAD_DIM, :] = values[
                lane, :, kv_head * HEAD_DIM : (kv_head + 1) * HEAD_DIM
            ].T
            values_t[lane, kv_head, HEAD_DIM:, :] = jnp.ones(
                (PADDED - HEAD_DIM, WINDOW), values_t.dtype
            )
    for lane in range(LANES):
        wait(1, lane)
    for copy in loads:
        copy.wait()

    @pl.loop(0, HEADS)
    def _(block):
        set_bias(block)
        reach = reach_ref[block]

        def run(skip, condition):
            @pl.when(condition)
            def _():
                for kv_head in range(kv_local):
                    total = part(
                        block, kv_head, kv_head * part_width, GROUP,
                        lambda scores, masks: scores * EXPONENT_SCALE + masks, skip,
                    )
                    inside = (total >= SMALL) & (total <= LARGE)
                    flags[...] = jnp.maximum(flags[...], jnp.where(inside, 0.0, 1.0))
                    store(block, kv_head).start()

        room = REACH * STRETCH
        low = 0
        for skip in SKIPS:
            run(skip, (reach > low) & (reach <= room - skip) if low else reach <= room - skip)
            low = room - skip

    for block in range(HEADS):
        for kv_head in range(kv_local):
            store(block, kv_head).wait()

    @pl.when(jnp.max(flags[...]) > 0)
    def _():
        def shifted(scores, masks):
            scores = scores + masks
            return (scores - jnp.max(scores, axis=0, keepdims=True)) * EXPONENT_SCALE

        @pl.loop(0, HEADS)
        def _(block):
            set_bias(block)
            for kv_head in range(kv_local):

                @pl.loop(0, GROUP)
                def _(head):
                    base = pl.multiple_of(kv_head * part_width + head * HEAD_DIM, HEAD_DIM)
                    part(block, kv_head, base, 1, shifted)

                copy = store(block, kv_head)
                copy.start()
                copy.wait()


def attention(
    count, place, starts, reach, own, up, down, far, inner, mate_up, mate_down,
    queries, left, right, across,
):
    rows, width = left.shape
    kv_width = own.shape[1] // 2
    kv_local = kv_width // HEAD_DIM
    dtype = queries.dtype
    return pl.pallas_call(
        functools.partial(attention_kernel, count),
        in_specs=[SMEM_SPEC, VMEM_SPEC, SMEM_SPEC] + [VMEM_SPEC] * 7 + [ANY_SPEC] * 4,
        out_specs=ANY_SPEC,
        out_shape=jax.ShapeDtypeStruct((HEADS * rows, width), dtype),
        scratch_shapes=[
            pltpu.VMEM((LANES, WINDOW, kv_width), dtype),
            pltpu.VMEM((LANES, WINDOW, kv_width), dtype),
            pltpu.VMEM((LANES, kv_local, PADDED, WINDOW), dtype),
            pltpu.VMEM((HEADS, rows, width), dtype),
            pltpu.VMEM((HEADS, rows, width), dtype),
            pltpu.VMEM((KEYS, ROWS), jnp.float32),
            pltpu.VMEM((1, GROUP * ROWS), jnp.float32),
            pltpu.SemaphoreType.DMA((2, LANES, REACH + 1)),
            pltpu.SemaphoreType.DMA((HEADS,)),
            pltpu.SemaphoreType.DMA((HEADS, kv_local)),
        ],
        compiler_params=PARAMS,
        name="attention",
    )(
        place, starts, reach, own, up, down, far, inner, mate_up, mate_down,
        queries, left, right, across,
    )


def body(queries, key_rows, value_rows, doc_lengths):
    count = lax.axis_size("ctx")
    ctx = lax.axis_index("ctx")
    odd = lax.rem(ctx, 2) == 1
    place = jnp.stack([ctx, lax.axis_index("head")])

    packed = kv_pack(key_rows, value_rows)
    to_next, to_previous, to_opposite, starts, reach = query_pack(count, place, doc_lengths.reshape(1, -1), queries)
    kv = lax.all_to_all(packed, "head", split_axis=0, concat_axis=0, tiled=True)
    kv = kv.reshape(LANES * STRETCH, -1)

    def rotate(block, shift):
        return lax.ppermute(block, "head", [(i, (i + shift) % HEADS) for i in range(HEADS)])

    kv, starts = lax.optimization_barrier((kv, starts))
    left = rotate(to_next, 1)
    right = rotate(to_previous, 3)
    across = rotate(to_opposite, 2)

    lane0, lane1 = kv[:STRETCH], kv[STRETCH:]
    last = ctx == count - 1
    swap = [(i, i ^ 1) for i in range(count)]
    up = lax.ppermute(lane0, "ctx", [(i, i + 2) for i in range(count - 2)])
    down = lax.ppermute(lane1, "ctx", [(i + 2, i) for i in range(count - 2)])
    route = [(i, i + 3) for i in range(1, count - 3, 2)]
    route += [(i + 3, i) for i in range(1, count - 3, 2)]
    route += [(count - 1, count - 3)]
    far = lax.ppermute(jnp.where(odd, lane0, lane1), "ctx", route)
    inner = lax.ppermute(jnp.where(odd, lane1, lane0), "ctx", swap)
    down, far, up, left, right = lax.optimization_barrier((down, far, up, left, right))
    mate_up = lax.ppermute(up, "ctx", swap)
    mate_down = lax.ppermute(jnp.where(last, lane0, down), "ctx", swap)
    return attention(
        count, place, starts, reach, kv, up, down, far, inner, mate_up, mate_down, queries, left, right, across
    )


def solution(mesh):
    placed = (P(("ctx", "head"), None), P(("ctx", "head"), None), P(("ctx", "head"), None), P())
    return jax.shard_map(
        body, mesh=mesh, in_specs=placed, out_specs=P("ctx", "head"), check_vma=False
    )
```
